32 devices in a mesh: gx: 2 (over x), gy: 4 (over z), col: 4 (over y, core).
Axes of the slice: x: 2, y: 2, z: 4, core: 2. Of those that a mesh axis runs over, the one named last changes fastest.
Arguments:
- right_side: float32 [8, 128, 512], P('gx', 'gy', 'col'), may hold values from -12 to 12
- diag_shift: float32 [8, 128, 512], P('gx', 'gy', 'col'), may hold values from 0.05 to 1
- stiffness: float32 [8, 128, 512], P('gx', 'gy', 'col'), may hold values from 0.5 to 2
- block_owner: int32 [32, 128], P(('gx', 'gy', 'col')), may hold values from 0 to 3, as said below
- block_group: int32 [32, 128], P(('gx', 'gy', 'col')), may hold values from 0 to 127
- coarse_inverse: float32 [32, 8, 128, 128], P(('gx', 'gy', 'col')), may hold values from -2e-05 to 0.0152
Outputs:
- solution_field: float32 [8, 128, 512], P('gx', 'gy', 'col')
- residual: float32 [8, 128, 512], P('gx', 'gy', 'col')
The draws below stay inside these ranges and needn't reach their ends.
Inputs may be any that keep to these rules, and one draw needn't show every extreme that they name: `block_owner`: the row blocks of one device name at most 64 blocks for one owner, and in every group of 4 devices that share gx and gy one owner gets exactly 64 blocks from each device of the group.
All inputs are finite; a program needn't handle non-finite values.
Results may differ from the reference program's by a relative error of at most 0.0003.
Values sent between devices are 32-bit elements; how exact they have to be, the bound alone decides.
No kernel may reach another device: no remote copies, remote signals or barrier semaphores. Data moves between devices by JAX's collectives and lax.ppermute only.
A program may use at most 64 MiB of HBM per device.

```python
import math
import jax
import jax.numpy as jnp
from jax import lax

CX = 4
CY = 32
CZ = 128
AGG = 16
ITERS = 4
NB = 128
CAP = 64
CG = 128
CB = 8
GROUPS = 8
NX = 8
NY = 128
NZ = 512
N_GX = 2
N_GY = 4
N_COL = 4
DEVICES = 32


def draw_right_side(key, part):
    key_normal = jax.random.fold_in(key, 0)
    grid_shape = (NX, NY, NZ)
    first_pos = lax.broadcasted_iota(jnp.float32, grid_shape, 0) / max(NX - 1, 1)
    second_pos = lax.broadcasted_iota(jnp.float32, grid_shape, 1) / max(NY - 1, 1)
    third_pos = lax.broadcasted_iota(jnp.float32, grid_shape, 2) / max(NZ - 1, 1)
    scaling = 0.5 * (1.0 + 0.75 * first_pos) * (1.0 + 0.75 * second_pos) * (1.0 + 0.75 * third_pos)
    base_field = jnp.clip(jax.random.normal(key_normal, grid_shape, jnp.float32), -4.0, 4.0)
    return base_field * scaling


def shuffle_row(row_key):
    return jax.random.permutation(row_key, NB)


def draw_block_owner(key, part):
    key_favour, key_other, key_order = jax.random.split(key, 3)
    favoured = jax.random.randint(key_favour, (DEVICES // N_COL,), 0, N_COL)
    favoured = jnp.repeat(favoured, N_COL)
    offsets = jax.random.randint(key_other, (DEVICES, NB - CAP), 1, N_COL)
    others = (favoured[:, None] + offsets) % N_COL
    rows_all = jnp.concatenate([jnp.broadcast_to(favoured[:, None], (DEVICES, CAP)), others], axis=1)
    orders = jax.vmap(shuffle_row)(jax.random.split(key_order, DEVICES))
    return jnp.take_along_axis(rows_all, orders, axis=1).astype(jnp.int32)


def draw_coarse_inverse(key, part):
    key_diag, key_noise = jax.random.split(key)
    diag_part = jnp.exp(jax.random.uniform(key_diag, (DEVICES, CB, 128), jnp.float32, jnp.log(0.003), jnp.log(0.012)))
    bound_off = 0.15 / 128.0
    noise = jax.random.uniform(key_noise, (DEVICES, CB, 128, 128), jnp.float32, -bound_off, bound_off)
    noise = 0.5 * (noise + jnp.swapaxes(noise, 2, 3))
    row_index = lax.broadcasted_iota(jnp.int32, (128, 128), 0)
    col_index = lax.broadcasted_iota(jnp.int32, (128, 128), 1)
    distance = jnp.abs(row_index - col_index).astype(jnp.float32)
    kernel = jnp.exp(distance * jnp.log(0.5))
    scales = jnp.sqrt(diag_part[:, :, :, None] * diag_part[:, :, None, :])
    return scales * (kernel[None, None] + noise)


def set_ends(entries, rng, smallest, top_value):
    longest = entries.shape.index(max(entries.shape))
    spots = []
    for shift in (0, 1):
        where = [jax.random.randint(jax.random.fold_in(rng, axis), (), 0, length) for axis, length in enumerate(entries.shape)]
        where[longest] = (where[longest] + shift) % entries.shape[longest]
        spots.append(tuple(where))
    return entries.at[spots[0]].set(smallest).at[spots[1]].set(top_value)


def block_levels(rng, extent, shards, least, largest):
    def one(axis_at, blocks):
        steps = jax.random.uniform(jax.random.fold_in(jax.random.fold_in(rng, 6), axis_at), (blocks,), jnp.float32, least / len(shards), largest / len(shards))
        return jnp.repeat(jnp.exp(steps), extent[axis_at] // blocks).reshape((-1,) + (1,) * (len(extent) - axis_at - 1))

    gain = one(*shards[0])
    for cut in shards[1:]:
        gain = gain * one(*cut)
    return gain


def setup_inputs(seed: int = 0) -> dict:
    key_list = jax.random.split(jax.random.key(seed), 7)
    return {
        "right_side": draw_right_side(jax.random.fold_in(key_list[6], 71), 0),
        "diag_shift": jnp.clip(jnp.exp(math.log(1.0) - 2.9957323 * jax.random.uniform(key_list[1], (NX, NY, NZ), jnp.float32) ** block_levels(key_list[1], (NX, NY, NZ), ((0, 2), (1, 4), (2, 4)), -0.2, 0.2)), 0.05, 1.0),
        "stiffness": jnp.clip(jnp.exp(math.log(2.0) - 1.3862944 * jax.random.uniform(key_list[2], (NX, NY, NZ), jnp.float32) ** block_levels(key_list[2], (NX, NY, NZ), ((0, 2), (1, 4), (2, 4)), -0.2, 0.2)), 0.5, 2.0),
        "block_owner": draw_block_owner(jax.random.fold_in(key_list[6], 71), 0),
        "block_group": set_ends(jax.random.randint(key_list[4], (DEVICES, NB), 0, NB), jax.random.fold_in(key_list[4], 1), 0, NB - 1).astype(jnp.int32),
        "coarse_inverse": draw_coarse_inverse(jax.random.fold_in(key_list[6], 71), 0),
    }


cheb_first = 1.0 / 1.7364
cheb_second = 1.0 / 0.4636
highest = lax.Precision.HIGHEST


def neighbour_sum(field):
    padded = jnp.pad(field, 1)
    total = padded[2:, 1:-1, 1:-1] + padded[:-2, 1:-1, 1:-1]
    total = total + padded[1:-1, 2:, 1:-1] + padded[1:-1, :-2, 1:-1]
    total = total + padded[1:-1, 1:-1, 2:] + padded[1:-1, 1:-1, :-2]
    return total


def to_blocks(field):
    shaped = field.reshape(N_GX, CX, N_GY, CY, N_COL, CZ).transpose(0, 2, 4, 1, 3, 5)
    return shaped.reshape(GROUPS, N_COL * NB, CZ)


def from_blocks(blocks):
    shaped = blocks.reshape(N_GX, N_GY, N_COL, CX, CY, CZ).transpose(0, 3, 1, 4, 2, 5)
    return shaped.reshape(NX, NY, NZ)


def group_sums(values, indices):
    return jax.ops.segment_sum(values, indices, num_segments=N_COL * CG)


def take_rows(table, indices):
    return jnp.take(table, indices, axis=0)


def reference(right_side, diag_shift, stiffness, block_owner, block_group, coarse_inverse):
    stiff_sum = neighbour_sum(stiffness)
    diagonal = diag_shift + stiffness * stiff_sum
    targets = (block_owner * CG + block_group).reshape(GROUPS, N_COL * NB).astype(jnp.int32)

    def operate(vector):
        return diag_shift * vector + stiffness * (stiff_sum * vector - neighbour_sum(stiffness * vector))

    def coarse(field):
        aggregates = to_blocks(field).reshape(GROUPS, N_COL * NB, CZ // AGG, AGG).sum(axis=3)
        coarse_rows = jax.vmap(group_sums)(aggregates, targets)
        solved = jnp.einsum("dbij,dbj->dbi", coarse_inverse, coarse_rows.reshape(DEVICES, CB, 128), precision=highest)
        solved = solved.reshape(GROUPS, N_COL * CG, CZ // AGG)
        chosen = jax.vmap(take_rows)(solved, targets)
        spread = jnp.broadcast_to(chosen[..., None], chosen.shape + (AGG,))
        return from_blocks(spread.reshape(GROUPS, N_COL * NB, CZ))

    def precondition(field):
        iterate = cheb_first * field / diagonal
        iterate = iterate + cheb_second * (field - operate(iterate)) / diagonal
        iterate = iterate + coarse(field - operate(iterate))
        iterate = iterate + cheb_second * (field - operate(iterate)) / diagonal
        iterate = iterate + cheb_first * (field - operate(iterate)) / diagonal
        return iterate

    solution_field = jnp.zeros_like(right_side)
    residual = right_side
    precond = precondition(residual)
    direction = precond
    gamma_now = jnp.sum(residual * precond)
    for iteration in range(ITERS):
        image_vec = operate(direction)
        alpha_step = gamma_now / jnp.sum(direction * image_vec)
        solution_field = solution_field + alpha_step * direction
        residual = residual - alpha_step * image_vec
        if iteration + 1 < ITERS:
            precond = precondition(residual)
            gamma_next = jnp.sum(residual * precond)
            direction = precond + (gamma_next / gamma_now) * direction
            gamma_now = gamma_next
    return solution_field, residual
```

```python
import functools

import jax
import jax.numpy as jnp
from jax import lax
from jax.experimental import pallas as pl
from jax.experimental.pallas import tpu as pltpu
from jax.sharding import PartitionSpec as P

AGG = 16
ITERS = 4
HALO = 16
LANES = 128
ALL = ("gx", "gy", "col")

w1 = 1.0 / 1.7364
w2 = 1.0 / 0.4636
f32 = jnp.float32


def iota(shape, dim):
    return lax.broadcasted_iota(jnp.int32, shape, dim)


def cross_sums(rows):
    n = rows[0].shape[0]
    lane = iota((n, LANES), 1)
    zero = jnp.zeros((n, LANES), f32)
    ahead = [pltpu.roll(x, 1, 1) for x in rows]
    behind = [pltpu.roll(x, LANES - 1, 1) for x in rows]
    out = []
    for c, x in enumerate(rows):
        left = jnp.where(lane == 0, ahead[c - 1] if c else zero, ahead[c])
        right = jnp.where(lane == LANES - 1, behind[c + 1] if c + 1 < len(rows) else zero, behind[c])
        out.append(left + right + pltpu.roll(x, 1, 0) + pltpu.roll(x, n - 1, 0))
    return out


class Sizes:
    def __init__(self, mesh_shape, cx, cy):
        self.gx, self.gy, self.col = mesh_shape
        self.devices = self.gx * self.gy * self.col
        self.cx, self.cy = cx, cy
        self.planes = self.gx * cx
        self.rows = cy + 2 * HALO
        self.nblock = cx * cy
        self.ngroup = self.nblock * (LANES // AGG) // LANES


def plane_sums(src, i, rows, z):
    mid = [src[i + 1, c, rows] for c in range(z.col)]
    return mid, [
        s + (src[i, c, rows] + src[i + 2, c, rows]) for c, s in enumerate(cross_sums(mid))
    ]


def clear_ends(ref, z):
    zero = jnp.zeros(ref.shape[1:], f32)
    ref[0] = zero
    ref[z.planes + 1] = zero


def each_plane(z, body):
    lax.fori_loop(0, z.planes, lambda i, carry: (body(i), carry)[1], 0)


def presmooth(rho, g, out, rows, z):
    c0, c1 = w1 * (1.0 - w2) + w2, w1 * w2

    def body(i):
        mid, total = plane_sums(rho, i, rows, z)
        for c in range(z.col):
            out[i + 1, c, rows] = c0 * mid[c] + c1 * (g[i, c, rows] * total[c])

    each_plane(z, body)


def smooth(src, rho, g, out, w, rows, z):
    def body(i):
        mid, total = plane_sums(src, i, rows, z)
        for c in range(z.col):
            out[i + 1, c, rows] = (1.0 - w) * mid[c] + w * (
                rho[i + 1, c, rows] + g[i, c, rows] * total[c]
            )

    each_plane(z, body)


def restrict_solve(rho, y2, g, s, hot, inv_t, parts, grouped, msg, rows, z):
    first = lax.axis_index("gx") * z.cx
    own = slice(HALO - rows.start, HALO - rows.start + z.cy)

    def body(k, carry):
        i = first + k
        mid, total = plane_sums(y2, i, rows, z)
        for c in range(z.col):
            gg = g[i, c, rows]
            left = (rho[i + 1, c, rows] - mid[c] + gg * total[c])[own]
            value = left * (s[i, c, rows][own] / gg[own])
            high = value.astype(jnp.bfloat16)
            rest = value - high.astype(f32)
            middle = rest.astype(jnp.bfloat16)
            low = (rest - middle.astype(f32)).astype(jnp.bfloat16)
            for n, part in enumerate((high, middle, low)):
                parts[n, c, k] = part
        return carry

    lax.fori_loop(0, z.cx, body, 0)
    total = jnp.zeros((z.nblock, LANES), f32)
    for n in range(3):
        flat = parts[n].reshape(z.col * z.nblock, LANES)
        total = total + jnp.dot(hot[...], flat, preferred_element_type=f32)
    grouped[...] = total
    per = LANES // AGG
    mask = (iota((per, LANES), 1) // AGG == iota((per, LANES), 0)).astype(f32)

    def solve(c, carry):
        acc = jnp.zeros((per, LANES), f32)
        for half in range(2):
            tile = grouped[pl.ds(pl.multiple_of(c * 16 + half * 8, 8), 8), :]
            for k in range(8):
                value = jnp.broadcast_to(tile[k : k + 1, :], (per, LANES)) * mask
                value = jnp.sum(value, axis=1, keepdims=True)
                acc = acc + value * inv_t[c, (half * 8 + k) * per : (half * 8 + k + 1) * per, :]
        msg[c] = jnp.sum(acc, axis=0, keepdims=True)
        return carry

    lax.fori_loop(0, z.ngroup, solve, 0)


def kernel_first(z, shifted, *refs):
    pieces = refs[: z.col]
    inv_t, g, s, targets, rho, y2, hot, out = refs[z.col : z.col + 8]
    wide, parts, grouped, msg = refs[z.col + 8 :]
    gx, col = lax.axis_index("gx"), lax.axis_index("col")
    clear_ends(wide, z)
    clear_ends(rho, z)
    clear_ends(y2, z)
    r = z.rows
    all_rows = slice(0, r)

    def place(p):
        if not shifted:
            return p
        q = p + gx * z.cx
        return jnp.where(q >= z.planes, q - z.planes, q)

    lane = iota((r, LANES), 1)
    row = iota((r, LANES), 0)

    def unpack(p):
        i = place(p)
        for m in range(z.col):
            c = col ^ m
            value = pieces[m][p, 2 * r : 3 * r, :]
            wide[i + 1, c] = value
            s[i, c] = value
            names = jnp.broadcast_to(pieces[m][p, 3 * r + 2 : 3 * r + 3, :], (r, LANES))
            names = jnp.sum(jnp.where(lane == row, names, 0.0), axis=1, keepdims=True)
            targets[i, c] = jnp.broadcast_to(names, (r, LANES)).astype(jnp.int32)

    each_plane(z, unpack)

    def coefficients(p):
        i = place(p)
        for m in range(z.col):
            c = col ^ m
            x = wide[i + 1, c]
            before = wide[i + 1, jnp.maximum(c - 1, 0)]
            after = wide[i + 1, jnp.minimum(c + 1, z.col - 1)]
            up = jnp.where(row == 0, pieces[m][p, 3 * r : 3 * r + 1, :], pltpu.roll(x, 1, 0))
            down = jnp.where(
                row == r - 1, pieces[m][p, 3 * r + 1 : 3 * r + 2, :], pltpu.roll(x, r - 1, 0)
            )
            left = jnp.where(lane == 0, pltpu.roll(before, 1, 1) * (c > 0).astype(f32), pltpu.roll(x, 1, 1))
            right = jnp.where(
                lane == LANES - 1,
                pltpu.roll(after, LANES - 1, 1) * (c < z.col - 1).astype(f32),
                pltpu.roll(x, LANES - 1, 1),
            )
            total = up + down + left + right + wide[i, c] + wide[i + 2, c]
            diagonal = pieces[m][p, r : 2 * r, :] + x * total
            inside = diagonal > 0.0
            scale = x / jnp.where(inside, diagonal, 1.0)
            scale = jnp.where(inside, scale, 0.0)
            g[i, c] = x * scale
            rho[i + 1, c] = pieces[m][p, 0:r, :] * scale

    each_plane(z, coefficients)
    group = iota((z.nblock, LANES), 0).astype(f32) + (col * z.nblock).astype(f32)
    for m in range(z.col):
        names = pieces[m][0, 3 * r + 3 : 3 * r + 4, :]
        hot[col ^ m] = (jnp.broadcast_to(names, (z.nblock, LANES)) == group).astype(jnp.bfloat16)
    presmooth(rho, g, y2, all_rows, z)
    hots = jnp.concatenate([hot[c] for c in range(z.col)], axis=1)
    restrict_solve(rho, y2, g, s, Whole(hots), inv_t, parts, grouped, msg, all_rows, z)
    for c in range(z.ngroup):
        out[:, c : c + 1, :] = jnp.broadcast_to(msg[c][None], (z.devices, 1, LANES))


class Whole:
    def __init__(self, value):
        self.value = value

    def __getitem__(self, key):
        return self.value


def prolong(recv, table, y2, s, targets, out, z, packed):
    n = z.ngroup
    if packed:

        def unpack(d, carry):
            for c in range(n):
                table[d, c : c + 1, :] = recv[d, :, c * LANES : (c + 1) * LANES]
            return carry

        lax.fori_loop(0, z.devices, unpack, 0)
    else:
        table = recv
    gy = lax.axis_index("gy")
    aggregate = iota((8, LANES), 1) // AGG

    def body(i):
        gx = i // z.cx
        for tile in range(z.rows // 8):
            rows = slice(tile * 8, tile * 8 + 8)
            side = -1 if tile * 8 < HALO else (1 if tile * 8 >= HALO + z.cy else 0)
            layer = jnp.clip(gy + side, 0, z.gy - 1)
            base = (gx * z.gy + layer) * z.col
            tables = [table[base + o] for o in range(z.col)]
            for c in range(z.col):
                t = targets[i, c, rows]
                line = t >> 4
                owner, block = line >> 3, line & 7
                picked = jnp.take_along_axis(tables[0], block, axis=0, mode="promise_in_bounds")
                for o in range(1, z.col):
                    other = jnp.take_along_axis(tables[o], block, axis=0, mode="promise_in_bounds")
                    picked = jnp.where(owner == o, other, picked)
                lane = (t & 15) * 8 + aggregate
                picked = jnp.take_along_axis(picked, lane, axis=1, mode="promise_in_bounds")
                out[i + 1, c, rows] = y2[i + 1, c, rows] + s[i, c, rows] * picked

    each_plane(z, body)


def weighted(a, b, h):
    return jnp.sum(jnp.sum(a * b * h, axis=(0, 1), keepdims=True)[0], axis=1, keepdims=True)


def kernel_next(z, step, *refs):
    first, last = step == 0, step == ITERS - 1
    names = ["recv", "g", "s", "targets", "rho", "y2", "hot", "inv_t"]
    if not first:
        names += ["state"]
    if step >= 2:
        names += ["old", "z_old"]
    outs = ["state_out", "out"]
    if not last:
        outs += ["w_out", "y2_out"]
    if step >= 1 and not last:
        outs += ["z_out"]
    if not first:
        outs += ["old_out"]
    scratch = ["ya", "yb", "table", "parts", "grouped", "msg"]
    k = dict(zip(names + outs + scratch, refs))
    g, s, rho = k["g"], k["s"], k["rho"]
    ya, yb, table = k["ya"], k["yb"], k["table"]
    clear_ends(ya, z)
    clear_ends(yb, z)
    wide_rows = slice(0, z.rows)
    trim = 8 if step >= 1 else 0
    rows = slice(trim, z.rows - trim)
    early = wide_rows if step <= 1 else rows
    prolong(k["recv"], table, k["y2"], s, k["targets"], ya, z, packed=not first)
    smooth(ya, rho, g, yb, w2, early, z)
    smooth(yb, rho, g, ya, w1, early, z)

    gx, col = lax.axis_index("gx"), lax.axis_index("col")
    own_rows = slice(HALO, HALO + z.cy)
    planes = pl.ds(gx * z.cx, z.cx)
    planes1 = pl.ds(gx * z.cx + 1, z.cx)
    h = 1.0 / g[planes, col, own_rows]
    w_new = k["w_out"] if not last else yb
    if first:
        clear_ends(w_new, z)

        def image(i):
            mid, total = plane_sums(ya, i, rows, z)
            for c in range(z.col):
                w_new[i + 1, c, rows] = mid[c] - g[i, c, rows] * total[c]

        each_plane(z, image)
        r, u, w = rho[planes1, col, own_rows], ya[planes1, col, own_rows], w_new[planes1, col, own_rows]
        k["state_out"][0] = r
        k["state_out"][1] = u
        dots = [weighted(r, u, h), weighted(w, u, h)]
    else:
        sums = jnp.zeros((1, LANES), f32)
        lo = z.ngroup * LANES

        def gather(d, acc):
            return acc + k["recv"][d, :, lo : lo + LANES]

        sums = lax.fori_loop(0, z.devices, gather, sums)
        lane1 = iota((1, LANES), 1)
        pick = lambda n: jnp.sum(jnp.where(lane1 == n, sums, 0.0), axis=1, keepdims=True)
        gamma, delta = pick(0), pick(1)
        k["old_out"][...] = jnp.broadcast_to(gamma, (1, LANES))
        if step == 1:
            beta = None
            alpha = gamma / delta
        else:
            beta = gamma / k["old"][0:1, 0:1]
            alpha = gamma / (delta + 2.0 * beta * pick(2) + beta * beta * pick(3))
        trim_new = w_new

        def image(i):
            mid, total = plane_sums(ya, i, rows, z)
            for c in range(z.col):
                n_vec = mid[c] - g[i, c, rows] * total[c]
                if beta is not None:
                    n_vec = n_vec + beta * k["z_old"][i, c, rows]
                if not last:
                    k["z_out"][i, c, rows] = n_vec
                trim_new[i + 1, c, rows] = rho[i + 1, c, rows] - alpha * n_vec

        w_now = rho[planes1, col, own_rows]
        m_now = ya[planes1, col, own_rows]
        if not last:
            clear_ends(w_new, z)
        each_plane(z, image)
        state, state_out = k["state"], k["state_out"]
        r, u = state[0], state[1]
        p, q, sv = u, m_now, w_now
        if beta is not None:
            p, q, sv = p + beta * state[2], q + beta * state[3], sv + beta * state[4]
            x = state[5] + alpha * p
        else:
            x = alpha * p
        r = r - alpha * sv
        u = u - alpha * q
        w = trim_new[planes1, col, own_rows]
        for n, value in enumerate((r, u, p, q, sv, x)):
            state_out[n] = value
        if last:
            state_out[6] = w
        dots = [weighted(r, u, h), weighted(w, u, h), weighted(sv, u, h), weighted(sv, p, h)]

    lane1 = iota((1, LANES), 1)
    line = jnp.zeros((1, LANES), f32)
    for n, value in enumerate(dots):
        line = jnp.where(lane1 == n, value, line)
    out = k["out"]
    if last:
        out[...] = jnp.broadcast_to(line[None], (z.devices, 1, LANES))
        return
    presmooth(w_new, g, k["y2_out"], rows, z)
    clear_ends(k["y2_out"], z)
    restrict_solve(
        w_new, k["y2_out"], g, s, k["hot"], k["inv_t"], k["parts"], k["grouped"], k["msg"], rows, z
    )
    for c in range(z.ngroup):
        out[:, :, c * LANES : (c + 1) * LANES] = jnp.broadcast_to(k["msg"][c][None], (z.devices, 1, LANES))
    lo = z.ngroup * LANES
    out[:, :, lo : lo + LANES] = jnp.broadcast_to(line[None], (z.devices, 1, LANES))


def kernel_last(z, recv, old, state, g, s, x_out, r_out):
    def gather(d, acc):
        return acc + recv[d]

    sums = lax.fori_loop(0, z.devices, gather, jnp.zeros((1, LANES), f32))
    lane1 = iota((1, LANES), 1)
    pick = lambda n: jnp.sum(jnp.where(lane1 == n, sums, 0.0), axis=1, keepdims=True)
    gamma, delta = pick(0), pick(1)
    beta = gamma / old[0:1, 0:1]
    alpha = gamma / (delta + 2.0 * beta * pick(2) + beta * beta * pick(3))
    gx, col = lax.axis_index("gx"), lax.axis_index("col")
    own_rows = slice(HALO, HALO + z.cy)
    for i in range(z.cx):
        gg = g[gx * z.cx + i, col, own_rows]
        ss = s[gx * z.cx + i, col, own_rows]
        p = state[1, i] + beta * state[2, i]
        sv = state[6, i] + beta * state[4, i]
        x_out[i] = (state[5, i] + alpha * p) / ss
        r_out[i] = (state[0, i] - alpha * sv) * (ss / gg)


def call(body, outs, scratch, *args, limit=None, name=None):
    vmem = pl.BlockSpec(memory_space=pltpu.VMEM)
    return pl.pallas_call(
        body,
        out_shape=outs,
        in_specs=[vmem] * len(args),
        out_specs=[vmem] * len(outs),
        scratch_shapes=scratch,
        compiler_params=pltpu.CompilerParams(vmem_limit_bytes=limit or 60 * 1024 * 1024),
        name=name,
    )(*args)


def gather_fields(z, right_side, diag_shift, stiffness, names):
    n_gx, n_gy, n_col = z.gx, z.gy, z.col
    grid_names = jnp.pad(names.reshape(z.cx, 1, z.cy), ((0, 0), (0, 0), (0, LANES - z.cy)))
    flat_names = jnp.broadcast_to(names.reshape(1, 1, z.nblock), (z.cx, 1, LANES))
    own = jnp.concatenate([right_side, diag_shift, stiffness, grid_names, flat_names], axis=1)

    def edge(part, a, b):
        lists = jnp.pad(
            names.reshape(z.cx, 1, z.cy)[:, :, a:b], ((0, 0), (0, 0), (0, LANES - HALO))
        )
        fields = [part(right_side, HALO), part(diag_shift, HALO), part(stiffness, HALO + 1)]
        return jnp.concatenate(fields + [lists], axis=1)

    head = edge(lambda f, n: f[:, :n], 0, HALO)
    tail = edge(lambda f, n: f[:, z.cy - n :], z.cy - HALO, z.cy)

    def pack(own, above, below):
        h = HALO
        n = z.cy
        lists = jnp.concatenate(
            [above[:, 3 * h + 1 :, :h], own[:, 3 * n : 3 * n + 1, :n], below[:, 3 * h + 1 :, :h]], axis=2
        )
        lists = jnp.pad(lists, ((0, 0), (0, 0), (0, LANES - z.rows)))
        return jnp.concatenate(
            [
                above[:, :h], own[:, :n], below[:, :h],
                above[:, h : 2 * h], own[:, n : 2 * n], below[:, h : 2 * h],
                above[:, 2 * h + 1 : 3 * h + 1], own[:, 2 * n : 3 * n], below[:, 2 * h : 3 * h],
                above[:, 2 * h : 2 * h + 1], below[:, 3 * h : 3 * h + 1],
                lists, own[:, 3 * n + 1 :], jnp.zeros((own.shape[0], 4, LANES), f32),
            ],
            axis=1,
        )

    def shift(value, step, swap):
        pairs = []
        for a in range(n_gx):
            for b in range(n_gy):
                if 0 <= b + step < n_gy:
                    pairs.append((a * n_gy + b, (a ^ swap) * n_gy + b + step))
        return lax.ppermute(value, ("gx", "gy"), pairs)

    if n_gx == 2:
        other = shift(own, 0, 1)
        above, below = shift(tail, 1, 0), shift(head, -1, 0)
        above2, below2 = shift(tail, 1, 1), shift(head, -1, 1)
        both = [pack(own, above, below), pack(other, above2, below2)]
        packed = jnp.concatenate(both, axis=0)
    else:
        packed = pack(own, shift(tail, 1, 0), shift(head, -1, 0))
        packed = lax.all_gather(packed, "gx", axis=0, tiled=True)
    pieces = [packed]
    for bit in (2, 1):
        pairs = [(i, i ^ bit) for i in range(n_col)]
        pieces = pieces + [lax.ppermute(piece, "col", pairs) for piece in pieces]
    return [pieces[0], pieces[2], pieces[1], pieces[3]]


def on_device(right_side, diag_shift, stiffness, block_owner, block_group, coarse_inverse):
    cx, cy, depth = right_side.shape
    z = Sizes([lax.axis_size(a) for a in ALL], cx, cy)
    names = (block_owner[0] * z.nblock + block_group[0]).astype(f32)
    pieces = gather_fields(z, right_side, diag_shift, stiffness, names)
    inv_t = jnp.swapaxes(coarse_inverse[0], 1, 2)

    shape = lambda *dims, dtype=f32: jax.ShapeDtypeStruct(dims, dtype)
    field = (z.planes, z.col, z.rows, LANES)
    padded = (z.planes + 2,) + field[1:]
    common = [
        pltpu.VMEM((3, z.col, z.cx, z.cy, LANES), jnp.bfloat16),
        pltpu.VMEM((z.nblock, LANES), f32),
        pltpu.VMEM((z.ngroup, 1, LANES), f32),
    ]
    g, s, targets, rho, y2, hot, msg = call(
        functools.partial(kernel_first, z, z.gx == 2),
        [
            shape(*field), shape(*field), shape(*field, dtype=jnp.int32), shape(*padded), shape(*padded),
            shape(z.col, z.nblock, LANES, dtype=jnp.bfloat16), shape(z.devices, z.ngroup, LANES),
        ],
        [pltpu.VMEM(padded, f32)] + common,
        *pieces, inv_t, name="begin",
    )
    hot = jnp.concatenate([hot[c] for c in range(z.col)], axis=1)
    swap = lambda m: lax.all_to_all(m, ALL, split_axis=0, concat_axis=0, tiled=True)
    state = old = z_old = None
    for step in range(ITERS):
        first, last = step == 0, step == ITERS - 1
        recv = swap(msg)
        args = [recv, g, s, targets, rho, y2, hot, inv_t]
        if not first:
            args += [state]
        if step >= 2:
            args += [old, z_old]
        width = (0 if last else z.ngroup * LANES) + LANES
        outs = [shape(7 if last else 6, cx, cy, LANES), shape(z.devices, 1, width)]
        if not last:
            outs += [shape(*padded), shape(*padded)]
        if step >= 1 and not last:
            outs += [shape(*field)]
        if not first:
            outs += [shape(1, LANES)]
        scratch = [pltpu.VMEM(padded, f32)] * 2 + [pltpu.VMEM((z.devices, z.ngroup, LANES), f32)] + common
        result = list(call(functools.partial(kernel_next, z, step), outs, scratch, *args, name=f"step{step}"))
        state, msg = result[:2]
        result = result[2:]
        if not last:
            rho, y2 = result[:2]
            result = result[2:]
        if step >= 1 and not last:
            z_old = result.pop(0)
        if not first:
            old = result.pop(0)
        else:
            old = None
    recv = swap(msg)
    x, r = call(
        functools.partial(kernel_last, z),
        [shape(cx, cy, LANES), shape(cx, cy, LANES)],
        [],
        recv, old, state, g, s, name="end",
    )
    return x, r


def solution(mesh):
    placed = (
        P("gx", "gy", "col"),
        P("gx", "gy", "col"),
        P("gx", "gy", "col"),
        P(("gx", "gy", "col"), None),
        P(("gx", "gy", "col"), None),
        P(("gx", "gy", "col"), None, None, None),
    )
    return jax.shard_map(
        on_device,
        mesh=mesh,
        in_specs=placed,
        out_specs=(P("gx", "gy", "col"), P("gx", "gy", "col")),
        check_vma=False,
    )
```

```python
import functools

import jax
import jax.numpy as jnp
from jax import lax
from jax.experimental import pallas as pl
from jax.experimental.pallas import tpu as pltpu
from jax.sharding import PartitionSpec as P

AGG = 16
ITERS = 4
HALO = 16
LANES = 128
ALL = ("gx", "gy", "col")

w1 = 1.0 / 1.7364
w2 = 1.0 / 0.4636
f32 = jnp.float32


def iota(shape, dim):
    return lax.broadcasted_iota(jnp.int32, shape, dim)


class Sizes:
    def __init__(self, mesh_shape, cx, cy):
        self.gx, self.gy, self.col = mesh_shape
        self.devices = self.gx * self.gy * self.col
        self.cx, self.cy = cx, cy
        self.planes = self.gx * cx
        self.rows = cy + 2 * HALO
        self.nblock = cx * cy
        self.ngroup = self.nblock * (LANES // AGG) // LANES


PAD = 8


def plain(t):
    return pl.ds(pl.multiple_of(t * 8, 8), 8)


def inner(t):
    return pl.ds(pl.multiple_of(t * 8 + PAD, 8), 8)


def row_sums(src, i, t, mid, z):
    lane = iota((8, LANES), 1)
    zero = jnp.zeros((8, LANES), f32)
    ahead = [pltpu.roll(x, 1, 1) for x in mid]
    behind = [pltpu.roll(x, LANES - 1, 1) for x in mid]
    out = []
    for c in range(z.col):
        left = jnp.where(lane == 0, ahead[c - 1] if c else zero, ahead[c])
        right = jnp.where(lane == LANES - 1, behind[c + 1] if c + 1 < z.col else zero, behind[c])
        up = src[i, c, pl.ds(t * 8 + PAD - 1, 8)]
        down = src[i, c, pl.ds(t * 8 + PAD + 1, 8)]
        out.append((left + right) + (up + down))
    return out


def sweep(src, tiles, z, visit):
    def body(t, carry):
        load = lambda i: [src[i, c, inner(t)] for c in range(z.col)]
        below, mid = load(0), load(1)
        for i in range(z.planes):
            above = load(i + 2)
            across = row_sums(src, i + 1, t, mid, z)
            for c in range(z.col):
                visit(i, t, c, mid[c], across[c] + (below[c] + above[c]))
            below, mid = mid, above
        return carry

    lax.fori_loop(tiles[0], tiles[1], body, 0)


def clear_ends(ref, z):
    zero = jnp.zeros(ref.shape[1:], f32)
    ref[0] = zero
    ref[z.planes + 1] = zero


def presmooth(rho, g, out, tiles, z):
    c0, c1 = w1 * (1.0 - w2) + w2, w1 * w2

    def visit(i, t, c, value, total):
        out[i + 1, c, inner(t)] = c0 * value + (c1 * g[i, c, plain(t)]) * total

    sweep(rho, tiles, z, visit)


def smooth(src, rho, g, out, w, tiles, z):
    def visit(i, t, c, value, total):
        out[i + 1, c, inner(t)] = (1.0 - w) * value + w * (
            rho[i + 1, c, inner(t)] + g[i, c, plain(t)] * total
        )

    sweep(src, tiles, z, visit)


def restrict_solve(rho, y2, g, s, hot, inv_t, parts, grouped, msg, z):
    first = lax.axis_index("gx") * z.cx
    col = lax.axis_index("col")

    def body(k, carry):
        i = first + k
        for j in range(z.cy // 8):
            t = HALO // 8 + j
            mid = [y2[i + 1, c, inner(t)] for c in range(z.col)]
            across = row_sums(y2, i + 1, t + 0 * k, mid, z)
            for c in range(z.col):
                total = across[c] + (y2[i, c, inner(t)] + y2[i + 2, c, inner(t)])
                gg = g[i, c, plain(t)]
                value = (rho[i + 1, c, inner(t)] - mid[c] + gg * total) * (s[i, c, plain(t)] / gg)
                high = value.astype(jnp.bfloat16).astype(f32)
                middle = (value - high).astype(jnp.bfloat16).astype(f32)
                low = value - high - middle
                for n, part in enumerate((high, middle, low)):
                    parts[n, c ^ col, k, j * 8 : j * 8 + 8] = part
        return carry

    lax.fori_loop(0, z.cx, body, 0)
    total = jnp.zeros((z.nblock, LANES), f32)
    for n in range(3):
        flat = parts[n].reshape(z.col * z.nblock, LANES).astype(jnp.bfloat16)
        total = total + jnp.dot(hot[...], flat, preferred_element_type=f32)
    grouped[...] = total
    per = LANES // AGG
    mask = (iota((per, LANES), 1) // AGG == iota((per, LANES), 0)).astype(f32)

    def solve(c, carry):
        acc = jnp.zeros((per, LANES), f32)
        for half in range(2):
            tile = grouped[pl.ds(pl.multiple_of(c * 16 + half * 8, 8), 8), :]
            for k in range(8):
                value = jnp.broadcast_to(tile[k : k + 1, :], (per, LANES)) * mask
                value = jnp.sum(value, axis=1, keepdims=True)
                acc = acc + value * inv_t[c, (half * 8 + k) * per : (half * 8 + k + 1) * per, :]
        msg[c] = jnp.sum(acc, axis=0, keepdims=True)
        return carry

    lax.fori_loop(0, z.ngroup, solve, 0)


def list_row(owner, group, z):
    return (owner[...] * z.nblock + group[...]).astype(f32)


def kernel_edges(z, r, d, s, owner, group, head, tail):
    h, n = HALO, z.cy
    names = list_row(owner, group, z)
    for out, rows, extra, first in ((head, slice(0, h), h, 0), (tail, slice(n - h, n), n - h - 1, n - h)):
        for k, field in enumerate((r, d, s)):
            out[:, k * h : (k + 1) * h] = field[:, rows]
        out[:, 3 * h : 3 * h + 8] = jnp.zeros((z.cx, 8, LANES), f32)
        out[:, 3 * h : 3 * h + 1] = s[:, extra : extra + 1]
        for i in range(z.cx):
            turn = (i * n + first) % LANES
            out[i, 3 * h + 1 : 3 * h + 2] = pltpu.roll(names, (LANES - turn) % LANES, 1) if turn else names


def kernel_pack(z, r, d, s, owner, group, above, below, out):
    h, n, m = HALO, z.cy, z.rows
    names = list_row(owner, group, z)
    lane = iota((1, LANES), 1)
    for k, field in enumerate((r, d, s)):
        out[:, k * m : k * m + h] = above[:, k * h : (k + 1) * h]
        out[:, k * m + h : k * m + h + n] = field[...]
        out[:, k * m + h + n : (k + 1) * m] = below[:, k * h : (k + 1) * h]
    out[:, 3 * m : 3 * m + 8] = jnp.zeros((z.cx, 8, LANES), f32)
    out[:, 3 * m : 3 * m + 1] = above[:, 3 * h : 3 * h + 1]
    out[:, 3 * m + 1 : 3 * m + 2] = below[:, 3 * h : 3 * h + 1]
    for i in range(z.cx):
        turn = (LANES + h - i * n) % LANES
        mine = pltpu.roll(names, turn, 1) if turn else names
        left = above[i, 3 * h + 1 : 3 * h + 2]
        right = pltpu.roll(below[i, 3 * h + 1 : 3 * h + 2], h + n, 1)
        out[i, 3 * m + 2 : 3 * m + 3] = jnp.where(lane < h, left, jnp.where(lane < h + n, mine, right))
        out[i, 3 * m + 3 : 3 * m + 4] = names


def kernel_first(z, layout, *refs):
    pieces = refs[: len(layout)]
    refs = refs[len(layout) :]
    inv_t, g, s, targets, rho, y2, hot, out = refs[:8]
    parts, grouped, msg = refs[8:]
    wide = y2
    gx, col = lax.axis_index("gx"), lax.axis_index("col")
    clear_ends(rho, z)
    clear_ends(y2, z)
    r = z.rows
    tiles = (0, r // 8)

    lane = iota((r, LANES), 1)
    row = iota((r, LANES), 0)

    def unpack(piece, c, i, p):
        rho[i + 1, c, PAD : PAD + r] = piece[p, 0:r]
        g[i, c] = piece[p, r : 2 * r]
        wide[i + 1, c, PAD : PAD + r] = piece[p, 2 * r : 3 * r]
        wide[i + 1, c, PAD - 1 : PAD] = piece[p, 3 * r : 3 * r + 1]
        wide[i + 1, c, PAD + r : PAD + r + 1] = piece[p, 3 * r + 1 : 3 * r + 2]
        names = jnp.broadcast_to(piece[p, 3 * r + 2 : 3 * r + 3], (r, LANES))
        names = jnp.sum(jnp.where(lane == row, names, 0.0), axis=1, keepdims=True)
        targets[i, c] = jnp.broadcast_to(names, (r, LANES)).astype(jnp.int32)

    for piece, (m, start, rotated) in zip(pieces, layout):

        def each(p, carry, piece=piece, m=m, start=start, rotated=rotated):
            i = p + start
            if rotated:
                i = i + gx * z.cx
                i = jnp.where(i >= z.planes, i - z.planes, i)
            unpack(piece, col ^ m, i, p)
            return carry

        lax.fori_loop(0, piece.shape[0], each, 0)

    def coefficients(i, t, c, x, total):
        diagonal = g[i, c, plain(t)] + x * total
        inside = diagonal > 0.0
        scale = jnp.where(inside, x / jnp.where(inside, diagonal, 1.0), 0.0)
        s[i, c, plain(t)] = x
        g[i, c, plain(t)] = x * scale
        rho[i + 1, c, inner(t)] = rho[i + 1, c, inner(t)] * scale

    sweep(wide, tiles, z, coefficients)
    group = iota((z.nblock, LANES), 0).astype(f32) + (col * z.nblock).astype(f32)
    for piece, (m, start, _) in zip(pieces, layout):
        if start:
            continue
        names = piece[0 if _ else gx * z.cx, 3 * r + 3 : 3 * r + 4, :].reshape(1, LANES)
        match = jnp.broadcast_to(names, (z.nblock, LANES)) == group
        hot[:, m * LANES : (m + 1) * LANES] = match.astype(jnp.bfloat16)
    presmooth(rho, g, y2, tiles, z)
    restrict_solve(rho, y2, g, s, hot, inv_t, parts, grouped, msg, z)
    for c in range(z.ngroup):
        out[:, c : c + 1, :] = jnp.broadcast_to(msg[c][None], (z.devices, 1, LANES))


def prolong(recv, table, y2, s, targets, out, tiles, z, packed):
    n = z.ngroup
    if packed:

        def unpack(d, carry):
            for c in range(n):
                table[d, c : c + 1, :] = recv[d, :, c * LANES : (c + 1) * LANES]
            return carry

        lax.fori_loop(0, z.devices, unpack, 0)
    else:
        table = recv
    gy = lax.axis_index("gy")
    aggregate = iota((8, LANES), 1) // AGG

    tiles = tuple(range(tiles[0], tiles[1]))

    def body(i, carry):
        gx = i // z.cx
        for tile in tiles:
            side = -1 if tile * 8 < HALO else (1 if tile * 8 >= HALO + z.cy else 0)
            layer = jnp.clip(gy + side, 0, z.gy - 1)
            base = (gx * z.gy + layer) * z.col
            tables = [table[base + o] for o in range(z.col)]
            for c in range(z.col):
                t = targets[i, c, plain(tile)]
                line = t >> 4
                owner, block = line >> 3, line & 7
                picked = jnp.take_along_axis(tables[0], block, axis=0, mode="promise_in_bounds")
                for o in range(1, z.col):
                    other = jnp.take_along_axis(tables[o], block, axis=0, mode="promise_in_bounds")
                    picked = jnp.where(owner == o, other, picked)
                lane = (t & 15) * 8 + aggregate
                picked = jnp.take_along_axis(picked, lane, axis=1, mode="promise_in_bounds")
                out[i + 1, c, inner(tile)] = y2[i + 1, c, inner(tile)] + s[i, c, plain(tile)] * picked
        return carry

    lax.fori_loop(0, z.planes, body, 0)


def weighted(a, b, h):
    return jnp.sum(jnp.sum(a * b * h, axis=(0, 1), keepdims=True)[0], axis=1, keepdims=True)


def kernel_next(z, step, *refs):
    first, last = step == 0, step == ITERS - 1
    names = ["recv", "g", "s", "targets", "rho", "y2", "hot", "inv_t"]
    if not first:
        names += ["state"]
    if step >= 2:
        names += ["old", "z_old"]
    outs = ["state_out", "out"]
    if not last:
        outs += ["w_out", "y2_out"]
    if step >= 1 and not last:
        outs += ["z_out"]
    if not first:
        outs += ["old_out"]
    scratch = ["table", "parts", "grouped", "msg"] + (["y2_out", "w_out"] if last else [])
    k = dict(zip(names + outs + scratch, refs))
    g, s, rho = k["g"], k["s"], k["rho"]
    ya, yb, table = k["y2_out"], k["w_out"], k["table"]
    clear_ends(ya, z)
    clear_ends(yb, z)
    trim = 1 if step >= 1 else 0
    rows = (trim, z.rows // 8 - trim)
    early = (0, z.rows // 8) if step <= 1 else rows
    prolong(k["recv"], table, k["y2"], s, k["targets"], ya, early, z, packed=not first)
    smooth(ya, rho, g, yb, w2, early, z)
    smooth(yb, rho, g, ya, w1, early, z)

    gx, col = lax.axis_index("gx"), lax.axis_index("col")
    own_rows = slice(HALO, HALO + z.cy)
    own_inner = slice(HALO + PAD, HALO + PAD + z.cy)
    planes = pl.ds(gx * z.cx, z.cx)
    planes1 = pl.ds(gx * z.cx + 1, z.cx)
    h = 1.0 / g[planes, col, own_rows]
    w_new = yb
    if first:

        def image(i, t, c, value, total):
            w_new[i + 1, c, inner(t)] = value - g[i, c, plain(t)] * total

        sweep(ya, rows, z, image)
        r, u, w = (ref[planes1, col, own_inner] for ref in (rho, ya, w_new))
        k["state_out"][0] = r
        k["state_out"][1] = u
        dots = [weighted(r, u, h), weighted(w, u, h)]
    else:
        sums = jnp.zeros((1, LANES), f32)
        lo = z.ngroup * LANES

        def gather(d, acc):
            return acc + k["recv"][d, :, lo : lo + LANES]

        sums = lax.fori_loop(0, z.devices, gather, sums)
        lane1 = iota((1, LANES), 1)
        pick = lambda n: jnp.sum(jnp.where(lane1 == n, sums, 0.0), axis=1, keepdims=True)
        gamma, delta = pick(0), pick(1)
        k["old_out"][...] = jnp.broadcast_to(gamma, (1, LANES))
        if step == 1:
            beta = None
            alpha = gamma / delta
        else:
            beta = gamma / k["old"][0:1, 0:1]
            alpha = gamma / (delta + 2.0 * beta * pick(2) + beta * beta * pick(3))

        def image(i, t, c, value, total):
            n_vec = value - g[i, c, plain(t)] * total
            if beta is not None:
                n_vec = n_vec + beta * k["z_old"][i, c, plain(t)]
            if not last:
                k["z_out"][i, c, plain(t)] = n_vec
            w_new[i + 1, c, inner(t)] = rho[i + 1, c, inner(t)] - alpha * n_vec

        w_now = rho[planes1, col, own_inner]
        m_now = ya[planes1, col, own_inner]
        sweep(ya, rows, z, image)
        state, state_out = k["state"], k["state_out"]
        r, u = state[0], state[1]
        p, q, sv = u, m_now, w_now
        if beta is not None:
            p, q, sv = p + beta * state[2], q + beta * state[3], sv + beta * state[4]
            x = state[5] + alpha * p
        else:
            x = alpha * p
        r = r - alpha * sv
        u = u - alpha * q
        w = w_new[planes1, col, own_inner]
        for n, value in enumerate((r, u, p, q, sv, x)):
            state_out[n] = value
        if last:
            state_out[6] = w
        dots = [weighted(r, u, h), weighted(w, u, h), weighted(sv, u, h), weighted(sv, p, h)]

    lane1 = iota((1, LANES), 1)
    line = jnp.zeros((1, LANES), f32)
    for n, value in enumerate(dots):
        line = jnp.where(lane1 == n, value, line)
    out = k["out"]
    if last:
        out[...] = jnp.broadcast_to(line[None], (z.devices, 1, LANES))
        return
    presmooth(w_new, g, k["y2_out"], rows, z)
    restrict_solve(
        w_new, k["y2_out"], g, s, k["hot"], k["inv_t"], k["parts"], k["grouped"], k["msg"], z
    )
    for c in range(z.ngroup):
        out[:, :, c * LANES : (c + 1) * LANES] = jnp.broadcast_to(k["msg"][c][None], (z.devices, 1, LANES))
    lo = z.ngroup * LANES
    out[:, :, lo : lo + LANES] = jnp.broadcast_to(line[None], (z.devices, 1, LANES))


def kernel_last(z, recv, old, state, g, s, x_out, r_out):
    def gather(d, acc):
        return acc + recv[d]

    sums = lax.fori_loop(0, z.devices, gather, jnp.zeros((1, LANES), f32))
    lane1 = iota((1, LANES), 1)
    pick = lambda n: jnp.sum(jnp.where(lane1 == n, sums, 0.0), axis=1, keepdims=True)
    gamma, delta = pick(0), pick(1)
    beta = gamma / old[0:1, 0:1]
    alpha = gamma / (delta + 2.0 * beta * pick(2) + beta * beta * pick(3))
    gx, col = lax.axis_index("gx"), lax.axis_index("col")
    own_rows = slice(HALO, HALO + z.cy)
    for i in range(z.cx):
        gg = g[gx * z.cx + i, col, own_rows]
        ss = s[gx * z.cx + i, col, own_rows]
        p = state[1, i] + beta * state[2, i]
        sv = state[6, i] + beta * state[4, i]
        x_out[i] = (state[5, i] + alpha * p) / ss
        r_out[i] = (state[0, i] - alpha * sv) * (ss / gg)


def call(z, body, outs, scratch, *args, name=None):
    room = 13 * (z.planes + 2) * z.col * z.rows * LANES * 4
    vmem = pl.BlockSpec(memory_space=pltpu.VMEM)
    return pl.pallas_call(
        body,
        out_shape=outs,
        in_specs=[vmem] * len(args),
        out_specs=[vmem] * len(outs),
        scratch_shapes=scratch,
        compiler_params=pltpu.CompilerParams(vmem_limit_bytes=min(room, 60 * 1024 * 1024)),
        name=name,
    )(*args)


def gather_fields(z, right_side, diag_shift, stiffness, owner, group):
    fields = (right_side, diag_shift, stiffness, owner, group)
    edge = jax.ShapeDtypeStruct((z.cx, 3 * HALO + 8, LANES), f32)
    head, tail = call(z, functools.partial(kernel_edges, z), [edge, edge], [], *fields, name="edges")
    above = lax.ppermute(tail, "gy", [(i, i + 1) for i in range(z.gy - 1)])
    below = lax.ppermute(head, "gy", [(i + 1, i) for i in range(z.gy - 1)])
    (packed,) = call(
        z, functools.partial(kernel_pack, z), [jax.ShapeDtypeStruct((z.cx, 3 * z.rows + 8, LANES), f32)],
        [], *fields, above, below, name="pack",
    )

    def turn(value, bit):
        return lax.ppermute(value, "col", [(i, i ^ bit) for i in range(z.col)])

    if z.gx == 2:
        swap = lambda value: lax.ppermute(value, "gx", [(0, 1), (1, 0)])
        cut = z.cx // 2
        across, beside = swap(packed), turn(packed, 2)
        corner_low, corner_high = turn(across[:cut], 2), swap(beside[cut:])
        pieces = [(packed, 0, 0), (across, 0, z.cx), (beside, 2, 0)]
        pieces += [(corner_low, 2, z.cx), (corner_high, 2, z.cx + cut)]
        rotated = True
    else:
        packed = lax.all_gather(packed, "gx", axis=0, tiled=True)
        pieces = [(packed, 0, 0), (turn(packed, 2), 2, 0)]
        rotated = False
    pieces = pieces + [(turn(value, 1), m ^ 1, start) for value, m, start in pieces]
    return [value for value, _, _ in pieces], [(m, start, rotated) for _, m, start in pieces]


def on_device(right_side, diag_shift, stiffness, block_owner, block_group, coarse_inverse):
    cx, cy, depth = right_side.shape
    z = Sizes([lax.axis_size(a) for a in ALL], cx, cy)
    pieces, layout = gather_fields(z, right_side, diag_shift, stiffness, block_owner, block_group)
    inv_t = jnp.swapaxes(coarse_inverse[0], 1, 2)

    shape = lambda *dims, dtype=f32: jax.ShapeDtypeStruct(dims, dtype)
    field = (z.planes, z.col, z.rows, LANES)
    padded = (z.planes + 2, z.col, z.rows + 2 * PAD, LANES)
    common = [
        pltpu.VMEM((3, z.col, z.cx, z.cy, LANES), f32),
        pltpu.VMEM((z.nblock, LANES), f32),
        pltpu.VMEM((z.ngroup, 1, LANES), f32),
    ]
    g, s, targets, rho, y2, hot, msg = call(
        z,
        functools.partial(kernel_first, z, layout),
        [
            shape(*field), shape(*field), shape(*field, dtype=jnp.int32), shape(*padded), shape(*padded),
            shape(z.nblock, z.col * LANES, dtype=jnp.bfloat16), shape(z.devices, z.ngroup, LANES),
        ],
        common,
        *pieces, inv_t, name="begin",
    )
    swap = lambda m: lax.all_to_all(m, ALL, split_axis=0, concat_axis=0, tiled=True)
    state = old = z_old = None
    for step in range(ITERS):
        first, last = step == 0, step == ITERS - 1
        recv = swap(msg)
        args = [recv, g, s, targets, rho, y2, hot, inv_t]
        if not first:
            args += [state]
        if step >= 2:
            args += [old, z_old]
        width = (0 if last else z.ngroup * LANES) + LANES
        outs = [shape(7 if last else 6, cx, cy, LANES), shape(z.devices, 1, width)]
        if not last:
            outs += [shape(*padded), shape(*padded)]
        if step >= 1 and not last:
            outs += [shape(*field)]
        if not first:
            outs += [shape(1, LANES)]
        scratch = [pltpu.VMEM((z.devices, z.ngroup, LANES), f32)] + common
        if last:
            scratch += [pltpu.VMEM(padded, f32)] * 2
        result = list(call(z, functools.partial(kernel_next, z, step), outs, scratch, *args, name=f"step{step}"))
        state, msg = result[:2]
        result = result[2:]
        if not last:
            rho, y2 = result[:2]
            result = result[2:]
        if step >= 1 and not last:
            z_old = result.pop(0)
        if not first:
            old = result.pop(0)
        else:
            old = None
    recv = swap(msg)
    x, r = call(
        z,
        functools.partial(kernel_last, z),
        [shape(cx, cy, LANES), shape(cx, cy, LANES)],
        [],
        recv, old, state, g, s, name="end",
    )
    return x, r


def solution(mesh):
    placed = (
        P("gx", "gy", "col"),
        P("gx", "gy", "col"),
        P("gx", "gy", "col"),
        P(("gx", "gy", "col"), None),
        P(("gx", "gy", "col"), None),
        P(("gx", "gy", "col"), None, None, None),
    )
    return jax.shard_map(
        on_device,
        mesh=mesh,
        in_specs=placed,
        out_specs=(P("gx", "gy", "col"), P("gx", "gy", "col")),
        check_vma=False,
    )
```

```python
import functools

import jax
import jax.numpy as jnp
from jax import lax
from jax.experimental import pallas as pl
from jax.experimental.pallas import tpu as pltpu
from jax.sharding import PartitionSpec as P

AGG = 16
ITERS = 4
HALO = 16
LANES = 128
ALL = ("gx", "gy", "col")

w1 = 1.0 / 1.7364
w2 = 1.0 / 0.4636
f32 = jnp.float32


def iota(shape, dim):
    return lax.broadcasted_iota(jnp.int32, shape, dim)


class Sizes:
    def __init__(self, mesh_shape, cx, cy):
        self.gx, self.gy, self.col = mesh_shape
        self.devices = self.gx * self.gy * self.col
        self.cx, self.cy = cx, cy
        self.planes = self.gx * cx
        self.small = self.planes <= 8
        self.rows = cy + 2 * HALO
        self.nblock = cx * cy
        self.ngroup = self.nblock * (LANES // AGG) // LANES


PAD = 8


def plain(t):
    return pl.ds(pl.multiple_of(t * 8, 8), 8)


def inner(t):
    return pl.ds(pl.multiple_of(t * 8 + PAD, 8), 8)


def row_sums(src, i, t, mid, z):
    lane = iota((8, LANES), 1)
    zero = jnp.zeros((8, LANES), f32)
    ahead = [pltpu.roll(x, 1, 1) for x in mid]
    behind = [pltpu.roll(x, LANES - 1, 1) for x in mid]
    out = []
    for c in range(z.col):
        left = jnp.where(lane == 0, ahead[c - 1] if c else zero, ahead[c])
        right = jnp.where(lane == LANES - 1, behind[c + 1] if c + 1 < z.col else zero, behind[c])
        up = src[i, c, pl.ds(t * 8 + PAD - 1, 8)]
        down = src[i, c, pl.ds(t * 8 + PAD + 1, 8)]
        out.append((left + right) + (up + down))
    return out


DELAY = 0


def loop(count, body, unroll):
    if unroll:
        for i in range(count):
            body(i, 0)
    else:
        lax.fori_loop(0, count, body, 0)


class Stores:
    def __init__(self):
        self.waiting = []

    def add(self, *stores):
        self.waiting.append(stores)
        if len(self.waiting) > DELAY:
            self.release()

    def release(self):
        for ref, where, value in self.waiting.pop(0):
            ref[where] = value

    def close(self):
        while self.waiting:
            self.release()


def sweep(src, tiles, z, visit):
    lo, hi = tiles
    each = hi - lo if z.small else 1

    def body(turn, carry):
        stores = Stores()
        for part in range(each):
            t = lo + turn * each + part
            load = lambda i: [src[i, c, inner(t)] for c in range(z.col)]
            below, mid = load(0), load(1)
            for i in range(z.planes):
                above = load(i + 2)
                across = row_sums(src, i + 1, t, mid, z)
                made = []
                for c in range(z.col):
                    made += visit(i, t, c, mid[c], across[c] + (below[c] + above[c]))
                stores.add(*made)
                below, mid = mid, above
        stores.close()
        return carry

    lax.fori_loop(0, (hi - lo) // each, body, 0)


def clear_ends(ref, z):
    zero = jnp.zeros(ref.shape[1:], f32)
    ref[0] = zero
    ref[z.planes + 1] = zero


def presmooth(rho, g, out, tiles, z):
    c0, c1 = w1 * (1.0 - w2) + w2, w1 * w2

    def visit(i, t, c, value, total):
        return [(out, (i + 1, c, inner(t)), c0 * value + (c1 * g[i, c, plain(t)]) * total)]

    sweep(rho, tiles, z, visit)


def smooth(src, rho, g, out, w, tiles, z):
    def visit(i, t, c, value, total):
        moved = rho[i + 1, c, inner(t)] + g[i, c, plain(t)] * total
        return [(out, (i + 1, c, inner(t)), (1.0 - w) * value + w * moved)]

    sweep(src, tiles, z, visit)


def restrict_solve(rho, y2, g, s, hot, inv_t, parts, grouped, msg, z):
    first = lax.axis_index("gx") * z.cx
    col = lax.axis_index("col")

    def body(k, carry):
        i = first + k
        stores = Stores()
        for j in range(z.cy // 8):
            t = HALO // 8 + j
            mid = [y2[i + 1, c, inner(t)] for c in range(z.col)]
            across = row_sums(y2, i + 1, t + 0 * k, mid, z)
            made = []
            for c in range(z.col):
                total = across[c] + (y2[i, c, inner(t)] + y2[i + 2, c, inner(t)])
                gg = g[i, c, plain(t)]
                value = (rho[i + 1, c, inner(t)] - mid[c] + gg * total) * (s[i, c, plain(t)] / gg)
                high = value.astype(jnp.bfloat16).astype(f32)
                middle = (value - high).astype(jnp.bfloat16).astype(f32)
                low = value - high - middle
                for n, part in enumerate((high, middle, low)):
                    made += [(parts, (n, c ^ col, k, slice(j * 8, j * 8 + 8)), part)]
            stores.add(*made)
        stores.close()
        return carry

    loop(z.cx, body, z.small)
    total = jnp.zeros((z.nblock, LANES), f32)
    for n in range(3):
        flat = parts[n].reshape(z.col * z.nblock, LANES).astype(jnp.bfloat16)
        total = total + jnp.dot(hot[...], flat, preferred_element_type=f32)
    grouped[...] = total
    per = LANES // AGG
    mask = (iota((per, LANES), 1) // AGG == iota((per, LANES), 0)).astype(f32)

    def solve(c, carry):
        acc = jnp.zeros((per, LANES), f32)
        for half in range(2):
            tile = grouped[pl.ds(c * 16 + half * 8, 8), :]
            for k in range(8):
                value = jnp.broadcast_to(tile[k : k + 1, :], (per, LANES)) * mask
                value = jnp.sum(value, axis=1, keepdims=True)
                acc = acc + value * inv_t[c, (half * 8 + k) * per : (half * 8 + k + 1) * per, :]
        msg[c] = jnp.sum(acc, axis=0, keepdims=True)
        return carry

    loop(z.ngroup, solve, z.small)


def list_row(owner, group, z):
    return (owner[...] * z.nblock + group[...]).astype(f32)


def kernel_edges(z, r, d, s, owner, group, head, tail):
    h, n = HALO, z.cy
    names = list_row(owner, group, z)
    for out, rows, extra, first in ((head, slice(0, h), h, 0), (tail, slice(n - h, n), n - h - 1, n - h)):
        for k, field in enumerate((r, d, s)):
            out[:, k * h : (k + 1) * h] = field[:, rows]
        out[:, 3 * h : 3 * h + 8] = jnp.zeros((z.cx, 8, LANES), f32)
        out[:, 3 * h : 3 * h + 1] = s[:, extra : extra + 1]
        for i in range(z.cx):
            turn = (i * n + first) % LANES
            out[i, 3 * h + 1 : 3 * h + 2] = pltpu.roll(names, (LANES - turn) % LANES, 1) if turn else names


def kernel_pack(z, r, d, s, owner, group, above, below, out):
    h, n, m = HALO, z.cy, z.rows
    names = list_row(owner, group, z)
    lane = iota((1, LANES), 1)
    for k, field in enumerate((r, d, s)):
        out[:, k * m : k * m + h] = above[:, k * h : (k + 1) * h]
        out[:, k * m + h : k * m + h + n] = field[...]
        out[:, k * m + h + n : (k + 1) * m] = below[:, k * h : (k + 1) * h]
    out[:, 3 * m : 3 * m + 8] = jnp.zeros((z.cx, 8, LANES), f32)
    out[:, 3 * m : 3 * m + 1] = above[:, 3 * h : 3 * h + 1]
    out[:, 3 * m + 1 : 3 * m + 2] = below[:, 3 * h : 3 * h + 1]
    for i in range(z.cx):
        turn = (LANES + h - i * n) % LANES
        mine = pltpu.roll(names, turn, 1) if turn else names
        left = above[i, 3 * h + 1 : 3 * h + 2]
        right = pltpu.roll(below[i, 3 * h + 1 : 3 * h + 2], h + n, 1)
        out[i, 3 * m + 2 : 3 * m + 3] = jnp.where(lane < h, left, jnp.where(lane < h + n, mine, right))
        out[i, 3 * m + 3 : 3 * m + 4] = names


def kernel_first(z, layout, *refs):
    pieces = refs[: len(layout)]
    refs = refs[len(layout) :]
    inv_t, g, s, targets, rho, y2, hot, out = refs[:8]
    parts, grouped, msg = refs[8:]
    wide = y2
    gx, col = lax.axis_index("gx"), lax.axis_index("col")
    clear_ends(rho, z)
    clear_ends(y2, z)
    r = z.rows
    tiles = (0, r // 8)

    lane = iota((r, LANES), 1)
    row = iota((r, LANES), 0)

    def unpack(piece, c, i, p):
        rho[i + 1, c, PAD : PAD + r] = piece[p, 0:r]
        g[i, c] = piece[p, r : 2 * r]
        wide[i + 1, c, PAD : PAD + r] = piece[p, 2 * r : 3 * r]
        wide[i + 1, c, PAD - 1 : PAD] = piece[p, 3 * r : 3 * r + 1]
        wide[i + 1, c, PAD + r : PAD + r + 1] = piece[p, 3 * r + 1 : 3 * r + 2]
        names = jnp.broadcast_to(piece[p, 3 * r + 2 : 3 * r + 3], (r, LANES))
        names = jnp.sum(jnp.where(lane == row, names, 0.0), axis=1, keepdims=True)
        targets[i, c] = jnp.broadcast_to(names, (r, LANES)).astype(jnp.int32)

    for piece, (m, start, rotated) in zip(pieces, layout):

        def each(p, carry, piece=piece, m=m, start=start, rotated=rotated):
            i = p + start
            if rotated:
                i = i + gx * z.cx
                i = jnp.where(i >= z.planes, i - z.planes, i)
            unpack(piece, col ^ m, i, p)
            return carry

        loop(piece.shape[0], each, z.small)

    def coefficients(i, t, c, x, total):
        diagonal = g[i, c, plain(t)] + x * total
        inside = diagonal > 0.0
        scale = jnp.where(inside, x / jnp.where(inside, diagonal, 1.0), 0.0)
        return [
            (s, (i, c, plain(t)), x),
            (g, (i, c, plain(t)), x * scale),
            (rho, (i + 1, c, inner(t)), rho[i + 1, c, inner(t)] * scale),
        ]

    sweep(wide, tiles, z, coefficients)
    group = iota((z.nblock, LANES), 0).astype(f32) + (col * z.nblock).astype(f32)
    for piece, (m, start, _) in zip(pieces, layout):
        if start:
            continue
        names = piece[0 if _ else gx * z.cx, 3 * r + 3 : 3 * r + 4, :].reshape(1, LANES)
        match = jnp.broadcast_to(names, (z.nblock, LANES)) == group
        hot[:, m * LANES : (m + 1) * LANES] = match.astype(jnp.bfloat16)
    presmooth(rho, g, y2, tiles, z)
    restrict_solve(rho, y2, g, s, hot, inv_t, parts, grouped, msg, z)
    for c in range(z.ngroup):
        out[:, c : c + 1, :] = jnp.broadcast_to(msg[c][None], (z.devices, 1, LANES))


def prolong(recv, table, y2, s, targets, out, tiles, z, packed):
    n = z.ngroup
    if packed:

        def unpack(d, carry):
            for c in range(n):
                table[d, c : c + 1, :] = recv[d, :, c * LANES : (c + 1) * LANES]
            return carry

        loop(z.devices, unpack, z.small)
    else:
        table = recv
    gy = lax.axis_index("gy")
    aggregate = iota((8, LANES), 1) // AGG

    tiles = tuple(range(tiles[0], tiles[1]))

    def body(i, carry):
        gx = i // z.cx
        stores = Stores()
        for tile in tiles:
            side = -1 if tile * 8 < HALO else (1 if tile * 8 >= HALO + z.cy else 0)
            layer = jnp.clip(gy + side, 0, z.gy - 1)
            base = (gx * z.gy + layer) * z.col
            tables = [table[base + o] for o in range(z.col)]
            made = []
            for c in range(z.col):
                t = targets[i, c, plain(tile)]
                line = t >> 4
                owner, block = line >> 3, line & 7
                picked = jnp.take_along_axis(tables[0], block, axis=0, mode="promise_in_bounds")
                for o in range(1, z.col):
                    other = jnp.take_along_axis(tables[o], block, axis=0, mode="promise_in_bounds")
                    picked = jnp.where(owner == o, other, picked)
                lane = (t & 15) * 8 + aggregate
                picked = jnp.take_along_axis(picked, lane, axis=1, mode="promise_in_bounds")
                value = y2[i + 1, c, inner(tile)] + s[i, c, plain(tile)] * picked
                made += [(out, (i + 1, c, inner(tile)), value)]
            stores.add(*made)
        stores.close()
        return carry

    loop(z.planes, body, z.small)


def weighted(a, b, h):
    return jnp.sum(jnp.sum(a * b * h, axis=(0, 1), keepdims=True)[0], axis=1, keepdims=True)


def kernel_next(z, step, *refs):
    first, last = step == 0, step == ITERS - 1
    names = ["recv", "g", "s", "targets", "rho", "y2", "hot", "inv_t"]
    if not first:
        names += ["state"]
    if step >= 2:
        names += ["old", "z_old"]
    outs = ["state_out", "out"]
    if not last:
        outs += ["w_out", "y2_out"]
    if step >= 1 and not last:
        outs += ["z_out"]
    if not first:
        outs += ["old_out"]
    scratch = ["table", "parts", "grouped", "msg"] + (["y2_out", "w_out"] if last else [])
    k = dict(zip(names + outs + scratch, refs))
    g, s, rho = k["g"], k["s"], k["rho"]
    ya, yb, table = k["y2_out"], k["w_out"], k["table"]
    clear_ends(ya, z)
    clear_ends(yb, z)
    trim = 1 if step >= 1 else 0
    rows = (trim, z.rows // 8 - trim)
    early = (0, z.rows // 8) if step <= 1 else rows
    prolong(k["recv"], table, k["y2"], s, k["targets"], ya, early, z, packed=not first)
    smooth(ya, rho, g, yb, w2, early, z)
    smooth(yb, rho, g, ya, w1, early, z)

    gx, col = lax.axis_index("gx"), lax.axis_index("col")
    own_rows = slice(HALO, HALO + z.cy)
    own_inner = slice(HALO + PAD, HALO + PAD + z.cy)
    planes = pl.ds(gx * z.cx, z.cx)
    planes1 = pl.ds(gx * z.cx + 1, z.cx)
    h = 1.0 / g[planes, col, own_rows]
    w_new = yb
    if first:

        def image(i, t, c, value, total):
            return [(w_new, (i + 1, c, inner(t)), value - g[i, c, plain(t)] * total)]

        sweep(ya, rows, z, image)
        r, u, w = (ref[planes1, col, own_inner] for ref in (rho, ya, w_new))
        k["state_out"][0] = r
        k["state_out"][1] = u
        dots = [weighted(r, u, h), weighted(w, u, h)]
    else:
        sums = jnp.zeros((1, LANES), f32)
        lo = z.ngroup * LANES

        def gather(d, acc):
            return acc + k["recv"][d, :, lo : lo + LANES]

        sums = lax.fori_loop(0, z.devices, gather, sums)
        lane1 = iota((1, LANES), 1)
        pick = lambda n: jnp.sum(jnp.where(lane1 == n, sums, 0.0), axis=1, keepdims=True)
        gamma, delta = pick(0), pick(1)
        k["old_out"][...] = jnp.broadcast_to(gamma, (1, LANES))
        if step == 1:
            beta = None
            alpha = gamma / delta
        else:
            beta = gamma / k["old"][0:1, 0:1]
            alpha = gamma / (delta + 2.0 * beta * pick(2) + beta * beta * pick(3))

        def image(i, t, c, value, total):
            n_vec = value - g[i, c, plain(t)] * total
            if beta is not None:
                n_vec = n_vec + beta * k["z_old"][i, c, plain(t)]
            made = [(w_new, (i + 1, c, inner(t)), rho[i + 1, c, inner(t)] - alpha * n_vec)]
            if not last:
                made += [(k["z_out"], (i, c, plain(t)), n_vec)]
            return made

        w_now = rho[planes1, col, own_inner]
        m_now = ya[planes1, col, own_inner]
        sweep(ya, rows, z, image)
        state, state_out = k["state"], k["state_out"]
        r, u = state[0], state[1]
        p, q, sv = u, m_now, w_now
        if beta is not None:
            p, q, sv = p + beta * state[2], q + beta * state[3], sv + beta * state[4]
            x = state[5] + alpha * p
        else:
            x = alpha * p
        r = r - alpha * sv
        u = u - alpha * q
        w = w_new[planes1, col, own_inner]
        for n, value in enumerate((r, u, p, q, sv, x)):
            state_out[n] = value
        if last:
            state_out[6] = w
        dots = [weighted(r, u, h), weighted(w, u, h), weighted(sv, u, h), weighted(sv, p, h)]

    lane1 = iota((1, LANES), 1)
    line = jnp.zeros((1, LANES), f32)
    for n, value in enumerate(dots):
        line = jnp.where(lane1 == n, value, line)
    out = k["out"]
    if last:
        out[...] = jnp.broadcast_to(line[None], (z.devices, 1, LANES))
        return
    presmooth(w_new, g, k["y2_out"], rows, z)
    restrict_solve(
        w_new, k["y2_out"], g, s, k["hot"], k["inv_t"], k["parts"], k["grouped"], k["msg"], z
    )
    for c in range(z.ngroup):
        out[:, :, c * LANES : (c + 1) * LANES] = jnp.broadcast_to(k["msg"][c][None], (z.devices, 1, LANES))
    lo = z.ngroup * LANES
    out[:, :, lo : lo + LANES] = jnp.broadcast_to(line[None], (z.devices, 1, LANES))


def kernel_last(z, recv, old, state, g, s, x_out, r_out):
    def gather(d, acc):
        return acc + recv[d]

    sums = lax.fori_loop(0, z.devices, gather, jnp.zeros((1, LANES), f32))
    lane1 = iota((1, LANES), 1)
    pick = lambda n: jnp.sum(jnp.where(lane1 == n, sums, 0.0), axis=1, keepdims=True)
    gamma, delta = pick(0), pick(1)
    beta = gamma / old[0:1, 0:1]
    alpha = gamma / (delta + 2.0 * beta * pick(2) + beta * beta * pick(3))
    gx, col = lax.axis_index("gx"), lax.axis_index("col")
    own_rows = slice(HALO, HALO + z.cy)
    for i in range(z.cx):
        gg = g[gx * z.cx + i, col, own_rows]
        ss = s[gx * z.cx + i, col, own_rows]
        p = state[1, i] + beta * state[2, i]
        sv = state[6, i] + beta * state[4, i]
        x_out[i] = (state[5, i] + alpha * p) / ss
        r_out[i] = (state[0, i] - alpha * sv) * (ss / gg)


def call(z, body, outs, scratch, *args, name=None):
    room = 13 * (z.planes + 2) * z.col * z.rows * LANES * 4
    vmem = pl.BlockSpec(memory_space=pltpu.VMEM)
    return pl.pallas_call(
        body,
        out_shape=outs,
        in_specs=[vmem] * len(args),
        out_specs=[vmem] * len(outs),
        scratch_shapes=scratch,
        compiler_params=pltpu.CompilerParams(vmem_limit_bytes=min(room, 60 * 1024 * 1024)),
        name=name,
    )(*args)


def gather_fields(z, right_side, diag_shift, stiffness, owner, group):
    fields = (right_side, diag_shift, stiffness, owner, group)
    edge = jax.ShapeDtypeStruct((z.cx, 3 * HALO + 8, LANES), f32)
    head, tail = call(z, functools.partial(kernel_edges, z), [edge, edge], [], *fields, name="edges")
    above = lax.ppermute(tail, "gy", [(i, i + 1) for i in range(z.gy - 1)])
    below = lax.ppermute(head, "gy", [(i + 1, i) for i in range(z.gy - 1)])
    (packed,) = call(
        z, functools.partial(kernel_pack, z), [jax.ShapeDtypeStruct((z.cx, 3 * z.rows + 8, LANES), f32)],
        [], *fields, above, below, name="pack",
    )

    def turn(value, bit):
        return lax.ppermute(value, "col", [(i, i ^ bit) for i in range(z.col)])

    if z.gx == 2:
        swap = lambda value: lax.ppermute(value, "gx", [(0, 1), (1, 0)])
        cut = z.cx // 2
        across, beside = swap(packed), turn(packed, 2)
        corner_low, corner_high = turn(across[:cut], 2), swap(beside[cut:])
        pieces = [(packed, 0, 0), (across, 0, z.cx), (beside, 2, 0)]
        pieces += [(corner_low, 2, z.cx), (corner_high, 2, z.cx + cut)]
        rotated = True
    else:
        packed = lax.all_gather(packed, "gx", axis=0, tiled=True)
        pieces = [(packed, 0, 0), (turn(packed, 2), 2, 0)]
        rotated = False
    pieces = pieces + [(turn(value, 1), m ^ 1, start) for value, m, start in pieces]
    return [value for value, _, _ in pieces], [(m, start, rotated) for _, m, start in pieces]


def on_device(right_side, diag_shift, stiffness, block_owner, block_group, coarse_inverse):
    cx, cy, depth = right_side.shape
    z = Sizes([lax.axis_size(a) for a in ALL], cx, cy)
    pieces, layout = gather_fields(z, right_side, diag_shift, stiffness, block_owner, block_group)
    inv_t = jnp.swapaxes(coarse_inverse[0], 1, 2)

    shape = lambda *dims, dtype=f32: jax.ShapeDtypeStruct(dims, dtype)
    field = (z.planes, z.col, z.rows, LANES)
    padded = (z.planes + 2, z.col, z.rows + 2 * PAD, LANES)
    common = [
        pltpu.VMEM((3, z.col, z.cx, z.cy, LANES), f32),
        pltpu.VMEM((z.nblock, LANES), f32),
        pltpu.VMEM((z.ngroup, 1, LANES), f32),
    ]
    g, s, targets, rho, y2, hot, msg = call(
        z,
        functools.partial(kernel_first, z, layout),
        [
            shape(*field), shape(*field), shape(*field, dtype=jnp.int32), shape(*padded), shape(*padded),
            shape(z.nblock, z.col * LANES, dtype=jnp.bfloat16), shape(z.devices, z.ngroup, LANES),
        ],
        common,
        *pieces, inv_t, name="begin",
    )
    swap = lambda m: lax.all_to_all(m, ALL, split_axis=0, concat_axis=0, tiled=True)
    state = old = z_old = None
    for step in range(ITERS):
        first, last = step == 0, step == ITERS - 1
        recv = swap(msg)
        args = [recv, g, s, targets, rho, y2, hot, inv_t]
        if not first:
            args += [state]
        if step >= 2:
            args += [old, z_old]
        width = (0 if last else z.ngroup * LANES) + LANES
        outs = [shape(7 if last else 6, cx, cy, LANES), shape(z.devices, 1, width)]
        if not last:
            outs += [shape(*padded), shape(*padded)]
        if step >= 1 and not last:
            outs += [shape(*field)]
        if not first:
            outs += [shape(1, LANES)]
        scratch = [pltpu.VMEM((z.devices, z.ngroup, LANES), f32)] + common
        if last:
            scratch += [pltpu.VMEM(padded, f32)] * 2
        result = list(call(z, functools.partial(kernel_next, z, step), outs, scratch, *args, name=f"step{step}"))
        state, msg = result[:2]
        result = result[2:]
        if not last:
            rho, y2 = result[:2]
            result = result[2:]
        if step >= 1 and not last:
            z_old = result.pop(0)
        if not first:
            old = result.pop(0)
        else:
            old = None
    recv = swap(msg)
    x, r = call(
        z,
        functools.partial(kernel_last, z),
        [shape(cx, cy, LANES), shape(cx, cy, LANES)],
        [],
        recv, old, state, g, s, name="end",
    )
    return x, r


def solution(mesh):
    placed = (
        P("gx", "gy", "col"),
        P("gx", "gy", "col"),
        P("gx", "gy", "col"),
        P(("gx", "gy", "col"), None),
        P(("gx", "gy", "col"), None),
        P(("gx", "gy", "col"), None, None, None),
    )
    return jax.shard_map(
        on_device,
        mesh=mesh,
        in_specs=placed,
        out_specs=(P("gx", "gy", "col"), P("gx", "gy", "col")),
        check_vma=False,
    )
```

```python
import functools

import jax
import jax.numpy as jnp
from jax import lax
from jax.experimental import pallas as pl
from jax.experimental.pallas import tpu as pltpu
from jax.sharding import PartitionSpec as P

AGG = 16
ITERS = 4
HALO = 16
LANES = 128
ALL = ("gx", "gy", "col")

w1 = 1.0 / 1.7364
w2 = 1.0 / 0.4636
f32 = jnp.float32


def iota(shape, dim):
    return lax.broadcasted_iota(jnp.int32, shape, dim)


class Sizes:
    def __init__(self, mesh_shape, cx, cy):
        self.gx, self.gy, self.col = mesh_shape
        self.devices = self.gx * self.gy * self.col
        self.cx, self.cy = cx, cy
        self.planes = self.gx * cx
        self.small = self.planes <= 8
        self.rows = cy + 2 * HALO
        self.nblock = cx * cy
        self.ngroup = self.nblock * (LANES // AGG) // LANES


PAD = 8


def plain(t):
    return pl.ds(pl.multiple_of(t * 8, 8), 8)


def inner(t):
    return pl.ds(pl.multiple_of(t * 8 + PAD, 8), 8)


def row_sums(src, i, t, mid, z):
    lane = iota((8, LANES), 1)
    zero = jnp.zeros((8, LANES), f32)
    ahead = [pltpu.roll(x, 1, 1) for x in mid]
    behind = [pltpu.roll(x, LANES - 1, 1) for x in mid]
    out = []
    for c in range(z.col):
        left = jnp.where(lane == 0, ahead[c - 1] if c else zero, ahead[c])
        right = jnp.where(lane == LANES - 1, behind[c + 1] if c + 1 < z.col else zero, behind[c])
        up = src[i, c, pl.ds(t * 8 + PAD - 1, 8)]
        down = src[i, c, pl.ds(t * 8 + PAD + 1, 8)]
        out.append((left + right) + (up + down))
    return out


DELAY = 0


def loop(count, body, unroll):
    if unroll:
        for i in range(count):
            body(i, 0)
    else:
        lax.fori_loop(0, count, body, 0)


class Stores:
    def __init__(self):
        self.waiting = []

    def add(self, *stores):
        self.waiting.append(stores)
        if len(self.waiting) > DELAY:
            self.release()

    def release(self):
        for ref, where, value in self.waiting.pop(0):
            ref[where] = value

    def close(self):
        while self.waiting:
            self.release()


def sweep(src, tiles, z, visit):
    lo, hi = tiles
    each = hi - lo if z.small else 1

    def body(turn, carry):
        stores = Stores()
        for part in range(each):
            t = lo + turn * each + part
            load = lambda i: [src[i, c, inner(t)] for c in range(z.col)]
            below, mid = load(0), load(1)
            for i in range(z.planes):
                above = load(i + 2)
                across = row_sums(src, i + 1, t, mid, z)
                made = []
                for c in range(z.col):
                    made += visit(i, t, c, mid[c], across[c] + (below[c] + above[c]))
                stores.add(*made)
                below, mid = mid, above
        stores.close()
        return carry

    lax.fori_loop(0, (hi - lo) // each, body, 0)


def clear_ends(ref, z):
    zero = jnp.zeros(ref.shape[1:], f32)
    ref[0] = zero
    ref[z.planes + 1] = zero


def presmooth(rho, g, out, tiles, z):
    c0, c1 = w1 * (1.0 - w2) + w2, w1 * w2

    def visit(i, t, c, value, total):
        return [(out, (i + 1, c, inner(t)), c0 * value + (c1 * g[i, c, plain(t)]) * total)]

    sweep(rho, tiles, z, visit)


def smooth(src, rho, g, out, w, tiles, z):
    def visit(i, t, c, value, total):
        moved = rho[i + 1, c, inner(t)] + g[i, c, plain(t)] * total
        return [(out, (i + 1, c, inner(t)), (1.0 - w) * value + w * moved)]

    sweep(src, tiles, z, visit)


def restrict_solve(rho, y2, g, s, hot, inv_t, parts, grouped, msg, z):
    first = lax.axis_index("gx") * z.cx
    col = lax.axis_index("col")

    def body(k, carry):
        i = first + k
        stores = Stores()
        for j in range(z.cy // 8):
            t = HALO // 8 + j
            mid = [y2[i + 1, c, inner(t)] for c in range(z.col)]
            across = row_sums(y2, i + 1, t + 0 * k, mid, z)
            made = []
            for c in range(z.col):
                total = across[c] + (y2[i, c, inner(t)] + y2[i + 2, c, inner(t)])
                gg = g[i, c, plain(t)]
                value = (rho[i + 1, c, inner(t)] - mid[c] + gg * total) * (s[i, c, plain(t)] / gg)
                high = value.astype(jnp.bfloat16).astype(f32)
                middle = (value - high).astype(jnp.bfloat16).astype(f32)
                low = value - high - middle
                for n, part in enumerate((high, middle, low)):
                    made += [(parts, (n, c ^ col, k, slice(j * 8, j * 8 + 8)), part)]
            stores.add(*made)
        stores.close()
        return carry

    loop(z.cx, body, z.small)
    total = jnp.zeros((z.nblock, LANES), f32)
    for n in range(3):
        flat = parts[n].reshape(z.col * z.nblock, LANES).astype(jnp.bfloat16)
        total = total + jnp.dot(hot[...], flat, preferred_element_type=f32)
    grouped[...] = total
    per = LANES // AGG
    mask = (iota((per, LANES), 1) // AGG == iota((per, LANES), 0)).astype(f32)

    def solve(c, carry):
        acc = jnp.zeros((per, LANES), f32)
        for half in range(2):
            tile = grouped[pl.ds(c * 16 + half * 8, 8), :]
            for k in range(8):
                value = jnp.broadcast_to(tile[k : k + 1, :], (per, LANES)) * mask
                value = jnp.sum(value, axis=1, keepdims=True)
                acc = acc + value * inv_t[c, (half * 8 + k) * per : (half * 8 + k + 1) * per, :]
        msg[c] = jnp.sum(acc, axis=0, keepdims=True)
        return carry

    loop(z.ngroup, solve, z.small)


def kernel_edges(z, block, head, tail, same):
    h, n = HALO, z.cy
    same[...] = block[...]
    for out, first, extra in ((head, 0, h), (tail, n - h, n - h - 1)):
        for k in range(3):
            out[:, k * h : (k + 1) * h] = block[:, k * n + first : k * n + first + h]
        out[:, 3 * h : 3 * h + 8] = block[:, 3 * n : 3 * n + 8]
        out[:, 3 * h : 3 * h + 1] = block[:, 2 * n + extra : 2 * n + extra + 1]


def kernel_halo(z, above, below, *refs):
    m = above.shape[1]
    outs = refs[len(refs) // 2 :] if len(refs) > 1 else refs
    blocks = refs[: len(refs) // 2] if len(refs) > 1 else ()
    for out in outs:
        for i in range(z.cx):
            out[2 * m * i : 2 * m * i + m] = above[i]
            out[2 * m * i + m : 2 * m * (i + 1)] = below[i]
    for out, block, first in zip(outs, blocks, (z.cx // 2, 0)):
        base, n = 2 * m * z.cx, block.shape[1]
        for k in range(z.cx // 2):
            out[base + k * n : base + (k + 1) * n] = block[first + k]


def kernel_first(z, blocks, halos, count, rotated, *refs):
    pieces = refs[:count]
    refs = refs[count:]
    inv_t, g, s, targets, rho, y2, hot, out = refs[:8]
    parts, grouped, msg = refs[8:]
    wide = y2
    gx, col = lax.axis_index("gx"), lax.axis_index("col")
    clear_ends(rho, z)
    clear_ends(y2, z)
    r = z.rows
    tiles = (0, r // 8)

    n, h = z.cy, HALO
    group = iota((z.nblock, LANES), 0).astype(f32) + (col * z.nblock).astype(f32)

    def place(p):
        if not rotated:
            return p
        i = p + gx * z.cx
        return jnp.where(i >= z.planes, i - z.planes, i)

    def spread(names, i, c, p, first, rows, at):
        shape = (rows, LANES)
        wanted = iota(shape, 1) == iota(shape, 0) + ((p % z.cx) * n + first)
        value = jnp.sum(jnp.where(wanted, jnp.broadcast_to(names, shape), 0.0), axis=1, keepdims=True)
        targets[i, c, at : at + rows] = jnp.broadcast_to(value, shape).astype(jnp.int32)

    for which, base, m, start, planes in blocks:

        def each(q, carry, piece=pieces[which], base=base, m=m, start=start):
            p = q + start
            i, c, row = place(p), col ^ m, base + q * (3 * n + 8)
            rho[i + 1, c, PAD + h : PAD + h + n] = piece[pl.ds(row, n)]
            g[i, c, h : h + n] = piece[pl.ds(row + n, n)]
            wide[i + 1, c, PAD + h : PAD + h + n] = piece[pl.ds(row + 2 * n, n)]
            spread(piece[pl.ds(row + 3 * n, 1)], i, c, p, 0, n, h)
            return carry

        loop(planes, each, z.small)
        if start == 0:
            shift = 0 if rotated else gx * (z.cx * (3 * n + 8))
            names = jnp.broadcast_to(pieces[which][pl.ds(base + shift + 3 * n, 1)], (z.nblock, LANES))
            hot[:, m * LANES : (m + 1) * LANES] = (names == group).astype(jnp.bfloat16)

    for which, base, m, start, planes in halos:

        def each(q, carry, piece=pieces[which], base=base, m=m, start=start):
            p = q + start
            i, c, row = place(p), col ^ m, base + q * (6 * h + 16)
            for top, first, edge, turn in ((row, 0, PAD - 1, n - h), (row + 3 * h + 8, h + n, PAD + r, 0)):
                rho[i + 1, c, PAD + first : PAD + first + h] = piece[pl.ds(top, h)]
                g[i, c, first : first + h] = piece[pl.ds(top + h, h)]
                wide[i + 1, c, PAD + first : PAD + first + h] = piece[pl.ds(top + 2 * h, h)]
                wide[i + 1, c, edge : edge + 1] = piece[pl.ds(top + 3 * h, 1)]
                spread(piece[pl.ds(top + 3 * h + 1, 1)], i, c, p, turn, h, first)
            return carry

        loop(planes, each, z.small)

    def coefficients(i, t, c, x, total):
        diagonal = g[i, c, plain(t)] + x * total
        inside = diagonal > 0.0
        scale = jnp.where(inside, x / jnp.where(inside, diagonal, 1.0), 0.0)
        return [
            (s, (i, c, plain(t)), x),
            (g, (i, c, plain(t)), x * scale),
            (rho, (i + 1, c, inner(t)), rho[i + 1, c, inner(t)] * scale),
        ]

    sweep(wide, tiles, z, coefficients)
    presmooth(rho, g, y2, tiles, z)
    restrict_solve(rho, y2, g, s, hot, inv_t, parts, grouped, msg, z)
    for c in range(z.ngroup):
        out[:, c : c + 1, :] = jnp.broadcast_to(msg[c][None], (z.devices, 1, LANES))


def prolong(recv, table, y2, s, targets, out, tiles, z, packed):
    n = z.ngroup
    if packed:

        def unpack(d, carry):
            for c in range(n):
                table[d, c : c + 1, :] = recv[d, :, c * LANES : (c + 1) * LANES]
            return carry

        loop(z.devices, unpack, z.small)
    else:
        table = recv
    gy = lax.axis_index("gy")
    aggregate = iota((8, LANES), 1) // AGG

    tiles = tuple(range(tiles[0], tiles[1]))

    def body(i, carry):
        gx = i // z.cx
        stores = Stores()
        for tile in tiles:
            side = -1 if tile * 8 < HALO else (1 if tile * 8 >= HALO + z.cy else 0)
            layer = jnp.clip(gy + side, 0, z.gy - 1)
            base = (gx * z.gy + layer) * z.col
            tables = [table[base + o] for o in range(z.col)]
            made = []
            for c in range(z.col):
                t = targets[i, c, plain(tile)]
                line = t >> 4
                owner, block = line >> 3, line & 7
                picked = jnp.take_along_axis(tables[0], block, axis=0, mode="promise_in_bounds")
                for o in range(1, z.col):
                    other = jnp.take_along_axis(tables[o], block, axis=0, mode="promise_in_bounds")
                    picked = jnp.where(owner == o, other, picked)
                lane = (t & 15) * 8 + aggregate
                picked = jnp.take_along_axis(picked, lane, axis=1, mode="promise_in_bounds")
                value = y2[i + 1, c, inner(tile)] + s[i, c, plain(tile)] * picked
                made += [(out, (i + 1, c, inner(tile)), value)]
            stores.add(*made)
        stores.close()
        return carry

    loop(z.planes, body, z.small)


def weighted(a, b, h):
    return jnp.sum(jnp.sum(a * b * h, axis=(0, 1), keepdims=True)[0], axis=1, keepdims=True)


def kernel_next(z, step, *refs):
    first, last = step == 0, step == ITERS - 1
    names = ["recv", "g", "s", "targets", "rho", "y2", "hot", "inv_t"]
    if not first:
        names += ["state"]
    if step >= 2:
        names += ["old", "z_old"]
    outs = ["state_out", "out"]
    if not last:
        outs += ["w_out", "y2_out"]
    if step >= 1 and not last:
        outs += ["z_out"]
    if not first:
        outs += ["old_out"]
    scratch = ["table", "parts", "grouped", "msg"] + (["y2_out", "w_out"] if last else [])
    k = dict(zip(names + outs + scratch, refs))
    g, s, rho = k["g"], k["s"], k["rho"]
    ya, yb, table = k["y2_out"], k["w_out"], k["table"]
    clear_ends(ya, z)
    clear_ends(yb, z)
    trim = 1 if step >= 1 else 0
    rows = (trim, z.rows // 8 - trim)
    early = (0, z.rows // 8) if step <= 1 else rows
    prolong(k["recv"], table, k["y2"], s, k["targets"], ya, early, z, packed=not first)
    smooth(ya, rho, g, yb, w2, early, z)
    smooth(yb, rho, g, ya, w1, early, z)

    gx, col = lax.axis_index("gx"), lax.axis_index("col")
    own_rows = slice(HALO, HALO + z.cy)
    own_inner = slice(HALO + PAD, HALO + PAD + z.cy)
    planes = pl.ds(gx * z.cx, z.cx)
    planes1 = pl.ds(gx * z.cx + 1, z.cx)
    h = 1.0 / g[planes, col, own_rows]
    w_new = yb
    if first:

        def image(i, t, c, value, total):
            return [(w_new, (i + 1, c, inner(t)), value - g[i, c, plain(t)] * total)]

        sweep(ya, rows, z, image)
        r, u, w = (ref[planes1, col, own_inner] for ref in (rho, ya, w_new))
        k["state_out"][0] = r
        k["state_out"][1] = u
        dots = [weighted(r, u, h), weighted(w, u, h)]
    else:
        sums = jnp.zeros((1, LANES), f32)
        lo = z.ngroup * LANES

        def gather(d, acc):
            return acc + k["recv"][d, :, lo : lo + LANES]

        sums = lax.fori_loop(0, z.devices, gather, sums)
        lane1 = iota((1, LANES), 1)
        pick = lambda n: jnp.sum(jnp.where(lane1 == n, sums, 0.0), axis=1, keepdims=True)
        gamma, delta = pick(0), pick(1)
        k["old_out"][...] = jnp.broadcast_to(gamma, (1, LANES))
        if step == 1:
            beta = None
            alpha = gamma / delta
        else:
            beta = gamma / k["old"][0:1, 0:1]
            alpha = gamma / (delta + 2.0 * beta * pick(2) + beta * beta * pick(3))

        def image(i, t, c, value, total):
            n_vec = value - g[i, c, plain(t)] * total
            if beta is not None:
                n_vec = n_vec + beta * k["z_old"][i, c, plain(t)]
            made = [(w_new, (i + 1, c, inner(t)), rho[i + 1, c, inner(t)] - alpha * n_vec)]
            if not last:
                made += [(k["z_out"], (i, c, plain(t)), n_vec)]
            return made

        w_now = rho[planes1, col, own_inner]
        m_now = ya[planes1, col, own_inner]
        sweep(ya, rows, z, image)
        state, state_out = k["state"], k["state_out"]
        r, u = state[0], state[1]
        p, q, sv = u, m_now, w_now
        if beta is not None:
            p, q, sv = p + beta * state[2], q + beta * state[3], sv + beta * state[4]
            x = state[5] + alpha * p
        else:
            x = alpha * p
        r = r - alpha * sv
        u = u - alpha * q
        w = w_new[planes1, col, own_inner]
        for n, value in enumerate((r, u, p, q, sv, x)):
            state_out[n] = value
        if last:
            state_out[6] = w
        dots = [weighted(r, u, h), weighted(w, u, h), weighted(sv, u, h), weighted(sv, p, h)]

    lane1 = iota((1, LANES), 1)
    line = jnp.zeros((1, LANES), f32)
    for n, value in enumerate(dots):
        line = jnp.where(lane1 == n, value, line)
    out = k["out"]
    if last:
        out[...] = jnp.broadcast_to(line[None], (z.devices, 1, LANES))
        return
    presmooth(w_new, g, k["y2_out"], rows, z)
    restrict_solve(
        w_new, k["y2_out"], g, s, k["hot"], k["inv_t"], k["parts"], k["grouped"], k["msg"], z
    )
    for c in range(z.ngroup):
        out[:, :, c * LANES : (c + 1) * LANES] = jnp.broadcast_to(k["msg"][c][None], (z.devices, 1, LANES))
    lo = z.ngroup * LANES
    out[:, :, lo : lo + LANES] = jnp.broadcast_to(line[None], (z.devices, 1, LANES))


def kernel_last(z, recv, old, state, g, s, x_out, r_out):
    def gather(d, acc):
        return acc + recv[d]

    sums = lax.fori_loop(0, z.devices, gather, jnp.zeros((1, LANES), f32))
    lane1 = iota((1, LANES), 1)
    pick = lambda n: jnp.sum(jnp.where(lane1 == n, sums, 0.0), axis=1, keepdims=True)
    gamma, delta = pick(0), pick(1)
    beta = gamma / old[0:1, 0:1]
    alpha = gamma / (delta + 2.0 * beta * pick(2) + beta * beta * pick(3))
    gx, col = lax.axis_index("gx"), lax.axis_index("col")
    own_rows = slice(HALO, HALO + z.cy)
    for i in range(z.cx):
        gg = g[gx * z.cx + i, col, own_rows]
        ss = s[gx * z.cx + i, col, own_rows]
        p = state[1, i] + beta * state[2, i]
        sv = state[6, i] + beta * state[4, i]
        x_out[i] = (state[5, i] + alpha * p) / ss
        r_out[i] = (state[0, i] - alpha * sv) * (ss / gg)


def call(z, body, outs, scratch, *args, name=None):
    room = 13 * (z.planes + 2) * z.col * z.rows * LANES * 4
    vmem = pl.BlockSpec(memory_space=pltpu.VMEM)
    return pl.pallas_call(
        body,
        out_shape=outs,
        in_specs=[vmem] * len(args),
        out_specs=[vmem] * len(outs),
        scratch_shapes=scratch,
        compiler_params=pltpu.CompilerParams(vmem_limit_bytes=min(room, 60 * 1024 * 1024)),
        name=name,
    )(*args)


def gather_fields(z, fields, inverse):
    cx, n, h = z.cx, 3 * z.cy + 8, 3 * HALO + 8
    shape = lambda *dims: jax.ShapeDtypeStruct(dims, f32)
    names = (fields[3] * z.nblock + fields[4]).astype(f32)
    block = jnp.concatenate(fields[:3] + (jnp.broadcast_to(names, (cx, 8, LANES)),), axis=1)
    edge = shape(cx, h, LANES)
    head, tail, block = call(
        z, functools.partial(kernel_edges, z), [edge, edge, shape(cx, n, LANES)], [], block, name="edges"
    )
    def neighbours():
        above = lax.ppermute(tail, "gy", [(i, i + 1) for i in range(z.gy - 1)])
        return above, lax.ppermute(head, "gy", [(i + 1, i) for i in range(z.gy - 1)])

    flat = lambda value: value.reshape(-1, LANES)

    def turn(value, bit):
        return lax.ppermute(value, "col", [(i, i ^ bit) for i in range(z.col)])

    halo = functools.partial(kernel_halo, z)
    if z.gx == 2:
        swap = lambda value: lax.ppermute(value, "gx", [(0, 1), (1, 0)])
        across, beside = swap(block), turn(block, 2)
        above, below = neighbours()
        above, inverse = lax.optimization_barrier((above, inverse))
        whole = shape(2 * cx * h + cx // 2 * n, LANES)
        to_x, to_y = call(z, halo, [whole, whole], [], above, below, beside, across, name="halo")
        from_x, from_y = swap(to_x), turn(to_y, 2)
        half = cx * h
        corner_low, corner_high = turn(from_x[:half], 2), swap(from_y[half : 2 * half])
        pieces = [flat(block), flat(across), flat(beside), to_x, from_x, from_y, corner_low, corner_high]
        end, cut = 2 * half, cx // 2
        blocks = [(0, 0, 0, 0, cx), (1, 0, 0, cx, cx), (2, 0, 2, 0, cx)]
        blocks += [(5, end, 2, cx, cut), (4, end, 2, cx + cut, cut)]
        halos = [(3, 0, 0, 0, cx), (4, 0, 0, cx, cx), (5, 0, 2, 0, cx)]
        halos += [(6, 0, 2, cx, cut), (7, 0, 2, cx + cut, cut)]
    else:
        above, below = neighbours()
        (edges,) = call(z, halo, [shape(2 * cx * h, LANES)], [], above, below, name="halo")
        pieces = [lax.all_gather(value, "gx", axis=0, tiled=True) for value in (flat(block), edges)]
        pieces += [turn(value, 2) for value in pieces]
        blocks = [(0, 0, 0, 0, z.planes), (2, 0, 2, 0, z.planes)]
        halos = [(1, 0, 0, 0, z.planes), (3, 0, 2, 0, z.planes)]
    count = len(pieces)
    pieces = pieces + [turn(value, 1) for value in pieces]
    mirror = lambda table: table + [(w + count, base, m ^ 1, a, b) for w, base, m, a, b in table]
    return pieces, (mirror(blocks), mirror(halos), 2 * count, z.gx == 2), inverse


def on_device(right_side, diag_shift, stiffness, block_owner, block_group, coarse_inverse):
    cx, cy, depth = right_side.shape
    z = Sizes([lax.axis_size(a) for a in ALL], cx, cy)
    fields = (right_side, diag_shift, stiffness, block_owner, block_group)
    pieces, layout, inv_t = gather_fields(z, fields, jnp.swapaxes(coarse_inverse[0], 1, 2))

    shape = lambda *dims, dtype=f32: jax.ShapeDtypeStruct(dims, dtype)
    field = (z.planes, z.col, z.rows, LANES)
    padded = (z.planes + 2, z.col, z.rows + 2 * PAD, LANES)
    common = [
        pltpu.VMEM((3, z.col, z.cx, z.cy, LANES), f32),
        pltpu.VMEM((z.nblock, LANES), f32),
        pltpu.VMEM((z.ngroup, 1, LANES), f32),
    ]
    g, s, targets, rho, y2, hot, msg = call(
        z,
        functools.partial(kernel_first, z, *layout),
        [
            shape(*field), shape(*field), shape(*field, dtype=jnp.int32), shape(*padded), shape(*padded),
            shape(z.nblock, z.col * LANES, dtype=jnp.bfloat16), shape(z.devices, z.ngroup, LANES),
        ],
        common,
        *pieces, inv_t, name="begin",
    )
    swap = lambda m: lax.all_to_all(m, ALL, split_axis=0, concat_axis=0, tiled=True)
    state = old = z_old = None
    for step in range(ITERS):
        first, last = step == 0, step == ITERS - 1
        recv = swap(msg)
        args = [recv, g, s, targets, rho, y2, hot, inv_t]
        if not first:
            args += [state]
        if step >= 2:
            args += [old, z_old]
        width = (0 if last else z.ngroup * LANES) + LANES
        outs = [shape(7 if last else 6, cx, cy, LANES), shape(z.devices, 1, width)]
        if not last:
            outs += [shape(*padded), shape(*padded)]
        if step >= 1 and not last:
            outs += [shape(*field)]
        if not first:
            outs += [shape(1, LANES)]
        scratch = [pltpu.VMEM((z.devices, z.ngroup, LANES), f32)] + common
        if last:
            scratch += [pltpu.VMEM(padded, f32)] * 2
        result = list(call(z, functools.partial(kernel_next, z, step), outs, scratch, *args, name=f"step{step}"))
        state, msg = result[:2]
        result = result[2:]
        if not last:
            rho, y2 = result[:2]
            result = result[2:]
        if step >= 1 and not last:
            z_old = result.pop(0)
        if not first:
            old = result.pop(0)
        else:
            old = None
    recv = swap(msg)
    x, r = call(
        z,
        functools.partial(kernel_last, z),
        [shape(cx, cy, LANES), shape(cx, cy, LANES)],
        [],
        recv, old, state, g, s, name="end",
    )
    return x, r


def solution(mesh):
    placed = (
        P("gx", "gy", "col"),
        P("gx", "gy", "col"),
        P("gx", "gy", "col"),
        P(("gx", "gy", "col"), None),
        P(("gx", "gy", "col"), None),
        P(("gx", "gy", "col"), None, None, None),
    )
    return jax.shard_map(
        on_device,
        mesh=mesh,
        in_specs=placed,
        out_specs=(P("gx", "gy", "col"), P("gx", "gy", "col")),
        check_vma=False,
    )
```

```python
import functools

import jax
import jax.numpy as jnp
from jax import lax
from jax.experimental import pallas as pl
from jax.experimental.pallas import tpu as pltpu
from jax.sharding import PartitionSpec as P

AGG = 16
ITERS = 4
HALO = 16
LANES = 128
ALL = ("gx", "gy", "col")

w1 = 1.0 / 1.7364
w2 = 1.0 / 0.4636
f32 = jnp.float32


def iota(shape, dim):
    return lax.broadcasted_iota(jnp.int32, shape, dim)


class Sizes:
    def __init__(self, mesh_shape, cx, cy):
        self.gx, self.gy, self.col = mesh_shape
        self.devices = self.gx * self.gy * self.col
        self.cx, self.cy = cx, cy
        self.planes = self.gx * cx
        self.small = self.planes <= 8
        self.rows = cy + 2 * HALO
        self.nblock = cx * cy
        self.ngroup = self.nblock * (LANES // AGG) // LANES


PAD = 8


def plain(t):
    return pl.ds(pl.multiple_of(t * 8, 8), 8)


def inner(t):
    return pl.ds(pl.multiple_of(t * 8 + PAD, 8), 8)


def row_sums(src, i, t, mid, z):
    lane = iota((8, LANES), 1)
    zero = jnp.zeros((8, LANES), f32)
    ahead = [pltpu.roll(x, 1, 1) for x in mid]
    behind = [pltpu.roll(x, LANES - 1, 1) for x in mid]
    out = []
    for c in range(z.col):
        left = jnp.where(lane == 0, ahead[c - 1] if c else zero, ahead[c])
        right = jnp.where(lane == LANES - 1, behind[c + 1] if c + 1 < z.col else zero, behind[c])
        up = src[i, c, pl.ds(t * 8 + PAD - 1, 8)]
        down = src[i, c, pl.ds(t * 8 + PAD + 1, 8)]
        out.append((left + right) + (up + down))
    return out


DELAY = 0


def loop(count, body, unroll):
    if unroll:
        for i in range(count):
            body(i, 0)
    else:
        lax.fori_loop(0, count, body, 0)


class Stores:
    def __init__(self):
        self.waiting = []

    def add(self, *stores):
        self.waiting.append(stores)
        if len(self.waiting) > DELAY:
            self.release()

    def release(self):
        for ref, where, value in self.waiting.pop(0):
            ref[where] = value

    def close(self):
        while self.waiting:
            self.release()


def first_plane(z, span):
    return lax.axis_index("gx") * (z.planes - span) if span else 0


def sweep(src, tiles, z, visit, span=None):
    lo, hi = tiles
    start = first_plane(z, span)
    each = hi - lo if z.small else 1

    def body(turn, carry):
        stores = Stores()
        for part in range(each):
            t = lo + turn * each + part
            load = lambda i: [src[i, c, inner(t)] for c in range(z.col)]
            below, mid = load(start), load(start + 1)
            for k in range(span or z.planes):
                i = start + k
                above = load(i + 2)
                across = row_sums(src, i + 1, t, mid, z)
                made = []
                for c in range(z.col):
                    made += visit(i, t, c, mid[c], across[c] + (below[c] + above[c]))
                stores.add(*made)
                below, mid = mid, above
        stores.close()
        return carry

    lax.fori_loop(0, (hi - lo) // each, body, 0)


def clear_ends(ref, z):
    zero = jnp.zeros(ref.shape[1:], f32)
    ref[0] = zero
    ref[z.planes + 1] = zero


def presmooth(rho, g, out, tiles, z):
    c0, c1 = w1 * (1.0 - w2) + w2, w1 * w2

    def visit(i, t, c, value, total):
        return [(out, (i + 1, c, inner(t)), c0 * value + (c1 * g[i, c, plain(t)]) * total)]

    sweep(rho, tiles, z, visit)


def smooth(src, rho, g, out, w, tiles, z, span=None):
    def visit(i, t, c, value, total):
        moved = rho[i + 1, c, inner(t)] + g[i, c, plain(t)] * total
        return [(out, (i + 1, c, inner(t)), (1.0 - w) * value + w * moved)]

    sweep(src, tiles, z, visit, span)


def restrict_solve(rho, y2, g, s, hot, inv_t, parts, grouped, msg, z):
    first = lax.axis_index("gx") * z.cx
    col = lax.axis_index("col")

    def body(k, carry):
        i = first + k
        stores = Stores()
        for j in range(z.cy // 8):
            t = HALO // 8 + j
            mid = [y2[i + 1, c, inner(t)] for c in range(z.col)]
            across = row_sums(y2, i + 1, t + 0 * k, mid, z)
            made = []
            for c in range(z.col):
                total = across[c] + (y2[i, c, inner(t)] + y2[i + 2, c, inner(t)])
                gg = g[i, c, plain(t)]
                value = (rho[i + 1, c, inner(t)] - mid[c] + gg * total) * (s[i, c, plain(t)] / gg)
                high = value.astype(jnp.bfloat16).astype(f32)
                middle = (value - high).astype(jnp.bfloat16).astype(f32)
                low = value - high - middle
                for n, part in enumerate((high, middle, low)):
                    made += [(parts, (n, c ^ col, k, slice(j * 8, j * 8 + 8)), part)]
            stores.add(*made)
        stores.close()
        return carry

    loop(z.cx, body, z.small)
    total = jnp.zeros((z.nblock, LANES), f32)
    for n in range(3):
        flat = parts[n].reshape(z.col * z.nblock, LANES).astype(jnp.bfloat16)
        total = total + jnp.dot(hot[...], flat, preferred_element_type=f32)
    grouped[...] = total
    per = LANES // AGG
    mask = (iota((per, LANES), 1) // AGG == iota((per, LANES), 0)).astype(f32)

    def solve(c, carry):
        acc = jnp.zeros((per, LANES), f32)
        for half in range(2):
            tile = grouped[pl.ds(c * 16 + half * 8, 8), :]
            for k in range(8):
                value = jnp.broadcast_to(tile[k : k + 1, :], (per, LANES)) * mask
                value = jnp.sum(value, axis=1, keepdims=True)
                acc = acc + value * inv_t[c, (half * 8 + k) * per : (half * 8 + k + 1) * per, :]
        msg[c] = jnp.sum(acc, axis=0, keepdims=True)
        return carry

    loop(z.ngroup, solve, z.small)


def kernel_edges(z, block, head, tail, same):
    h, n = HALO, z.cy
    same[...] = block[...]
    for out, first, extra in ((head, 0, h), (tail, n - h, n - h - 1)):
        for k in range(3):
            out[:, k * h : (k + 1) * h] = block[:, k * n + first : k * n + first + h]
        out[:, 3 * h : 3 * h + 8] = block[:, 3 * n : 3 * n + 8]
        out[:, 3 * h : 3 * h + 1] = block[:, 2 * n + extra : 2 * n + extra + 1]


def kernel_halo(z, above, below, *refs):
    m = above.shape[1]
    outs = refs[len(refs) // 2 :] if len(refs) > 1 else refs
    blocks = refs[: len(refs) // 2] if len(refs) > 1 else ()
    for out in outs:
        for i in range(z.cx):
            out[2 * m * i : 2 * m * i + m] = above[i]
            out[2 * m * i + m : 2 * m * (i + 1)] = below[i]
    for out, block, first in zip(outs, blocks, (z.cx // 2, 0)):
        base, n = 2 * m * z.cx, block.shape[1]
        for k in range(z.cx // 2):
            out[base + k * n : base + (k + 1) * n] = block[first + k]


def kernel_first(z, blocks, halos, count, rotated, *refs):
    pieces = refs[:count]
    refs = refs[count:]
    inv_t, g, s, targets, rho, y2, hot, out = refs[:8]
    parts, grouped, msg = refs[8:]
    wide = y2
    gx, col = lax.axis_index("gx"), lax.axis_index("col")
    clear_ends(rho, z)
    clear_ends(y2, z)
    r = z.rows
    tiles = (0, r // 8)

    n, h = z.cy, HALO
    group = iota((z.nblock, LANES), 0).astype(f32) + (col * z.nblock).astype(f32)

    def place(p):
        if not rotated:
            return p
        i = p + gx * z.cx
        return jnp.where(i >= z.planes, i - z.planes, i)

    def spread(names, i, c, p, first, rows, at):
        shape = (rows, LANES)
        wanted = iota(shape, 1) == iota(shape, 0) + ((p % z.cx) * n + first)
        value = jnp.sum(jnp.where(wanted, jnp.broadcast_to(names, shape), 0.0), axis=1, keepdims=True)
        targets[i, c, at : at + rows] = jnp.broadcast_to(value, shape).astype(jnp.int32)

    for which, base, m, start, planes in blocks:

        def each(q, carry, piece=pieces[which], base=base, m=m, start=start):
            p = q + start
            i, c, row = place(p), col ^ m, base + q * (3 * n + 8)
            rho[i + 1, c, PAD + h : PAD + h + n] = piece[pl.ds(row, n)]
            g[i, c, h : h + n] = piece[pl.ds(row + n, n)]
            wide[i + 1, c, PAD + h : PAD + h + n] = piece[pl.ds(row + 2 * n, n)]
            spread(piece[pl.ds(row + 3 * n, 1)], i, c, p, 0, n, h)
            return carry

        loop(planes, each, z.small)
        if start == 0:
            shift = 0 if rotated else gx * (z.cx * (3 * n + 8))
            names = jnp.broadcast_to(pieces[which][pl.ds(base + shift + 3 * n, 1)], (z.nblock, LANES))
            hot[:, m * LANES : (m + 1) * LANES] = (names == group).astype(jnp.bfloat16)

    for which, base, m, start, planes in halos:

        def each(q, carry, piece=pieces[which], base=base, m=m, start=start):
            p = q + start
            i, c, row = place(p), col ^ m, base + q * (6 * h + 16)
            for top, first, edge, turn in ((row, 0, PAD - 1, n - h), (row + 3 * h + 8, h + n, PAD + r, 0)):
                rho[i + 1, c, PAD + first : PAD + first + h] = piece[pl.ds(top, h)]
                g[i, c, first : first + h] = piece[pl.ds(top + h, h)]
                wide[i + 1, c, PAD + first : PAD + first + h] = piece[pl.ds(top + 2 * h, h)]
                wide[i + 1, c, edge : edge + 1] = piece[pl.ds(top + 3 * h, 1)]
                spread(piece[pl.ds(top + 3 * h + 1, 1)], i, c, p, turn, h, first)
            return carry

        loop(planes, each, z.small)

    def coefficients(i, t, c, x, total):
        diagonal = g[i, c, plain(t)] + x * total
        inside = diagonal > 0.0
        scale = jnp.where(inside, x / jnp.where(inside, diagonal, 1.0), 0.0)
        return [
            (s, (i, c, plain(t)), x),
            (g, (i, c, plain(t)), x * scale),
            (rho, (i + 1, c, inner(t)), rho[i + 1, c, inner(t)] * scale),
        ]

    sweep(wide, tiles, z, coefficients)
    presmooth(rho, g, y2, tiles, z)
    restrict_solve(rho, y2, g, s, hot, inv_t, parts, grouped, msg, z)
    for c in range(z.ngroup):
        out[:, c : c + 1, :] = jnp.broadcast_to(msg[c][None], (z.devices, 1, LANES))


def prolong(recv, table, y2, s, targets, out, tiles, z, packed, span=None):
    n = z.ngroup
    if packed:

        def unpack(d, carry):
            for c in range(n):
                table[d, c : c + 1, :] = recv[d, :, c * LANES : (c + 1) * LANES]
            return carry

        loop(z.devices, unpack, z.small)
    else:
        table = recv
    gy = lax.axis_index("gy")
    aggregate = iota((8, LANES), 1) // AGG

    tiles = tuple(range(tiles[0], tiles[1]))

    start = first_plane(z, span)

    def body(k, carry):
        i = start + k
        gx = i // z.cx
        stores = Stores()
        for tile in tiles:
            side = -1 if tile * 8 < HALO else (1 if tile * 8 >= HALO + z.cy else 0)
            layer = jnp.clip(gy + side, 0, z.gy - 1)
            base = (gx * z.gy + layer) * z.col
            tables = [table[base + o] for o in range(z.col)]
            made = []
            for c in range(z.col):
                t = targets[i, c, plain(tile)]
                line = t >> 4
                owner, block = line >> 3, line & 7
                picked = jnp.take_along_axis(tables[0], block, axis=0, mode="promise_in_bounds")
                for o in range(1, z.col):
                    other = jnp.take_along_axis(tables[o], block, axis=0, mode="promise_in_bounds")
                    picked = jnp.where(owner == o, other, picked)
                lane = (t & 15) * 8 + aggregate
                picked = jnp.take_along_axis(picked, lane, axis=1, mode="promise_in_bounds")
                value = y2[i + 1, c, inner(tile)] + s[i, c, plain(tile)] * picked
                made += [(out, (i + 1, c, inner(tile)), value)]
            stores.add(*made)
        stores.close()
        return carry

    loop(span or z.planes, body, z.small)


def weighted(a, b, h):
    return jnp.sum(jnp.sum(a * b * h, axis=(0, 1), keepdims=True)[0], axis=1, keepdims=True)


def kernel_next(z, step, *refs):
    first, last = step == 0, step == ITERS - 1
    names = ["recv", "g", "s", "targets", "rho", "y2", "hot", "inv_t"]
    if not first:
        names += ["state"]
    if step >= 2:
        names += ["old", "z_old"]
    outs = ["state_out", "out"]
    if not last:
        outs += ["w_out", "y2_out"]
    if step >= 1 and not last:
        outs += ["z_out"]
    if not first:
        outs += ["old_out"]
    scratch = ["table", "parts", "grouped", "msg"] + (["y2_out", "w_out"] if last else [])
    k = dict(zip(names + outs + scratch, refs))
    g, s, rho = k["g"], k["s"], k["rho"]
    ya, yb, table = k["y2_out"], k["w_out"], k["table"]
    clear_ends(ya, z)
    clear_ends(yb, z)
    trim = 1 if step >= 1 else 0
    rows = (trim, z.rows // 8 - trim)
    early = (0, z.rows // 8) if step <= 1 else rows
    spans = [None] * 4
    if last:
        rows = (HALO // 8, (HALO + z.cy) // 8)
        if z.gx == 2 and z.cx > 3:
            spans = [z.cx + n for n in (3, 2, 1, 0)]
    prolong(k["recv"], table, k["y2"], s, k["targets"], ya, early, z, not first, spans[0])
    smooth(ya, rho, g, yb, w2, early, z, spans[1])
    smooth(yb, rho, g, ya, w1, early, z, spans[2])

    gx, col = lax.axis_index("gx"), lax.axis_index("col")
    own_rows = slice(HALO, HALO + z.cy)
    own_inner = slice(HALO + PAD, HALO + PAD + z.cy)
    planes = pl.ds(gx * z.cx, z.cx)
    planes1 = pl.ds(gx * z.cx + 1, z.cx)
    h = 1.0 / g[planes, col, own_rows]
    w_new = yb
    if first:

        def image(i, t, c, value, total):
            return [(w_new, (i + 1, c, inner(t)), value - g[i, c, plain(t)] * total)]

        sweep(ya, rows, z, image)
        r, u, w = (ref[planes1, col, own_inner] for ref in (rho, ya, w_new))
        k["state_out"][0] = r
        k["state_out"][1] = u
        dots = [weighted(r, u, h), weighted(w, u, h)]
    else:
        sums = jnp.zeros((1, LANES), f32)
        lo = z.ngroup * LANES

        def gather(d, acc):
            return acc + k["recv"][d, :, lo : lo + LANES]

        sums = lax.fori_loop(0, z.devices, gather, sums)
        lane1 = iota((1, LANES), 1)
        pick = lambda n: jnp.sum(jnp.where(lane1 == n, sums, 0.0), axis=1, keepdims=True)
        gamma, delta = pick(0), pick(1)
        k["old_out"][...] = jnp.broadcast_to(gamma, (1, LANES))
        if step == 1:
            beta = None
            alpha = gamma / delta
        else:
            beta = gamma / k["old"][0:1, 0:1]
            alpha = gamma / (delta + 2.0 * beta * pick(2) + beta * beta * pick(3))

        def image(i, t, c, value, total):
            n_vec = value - g[i, c, plain(t)] * total
            if beta is not None:
                n_vec = n_vec + beta * k["z_old"][i, c, plain(t)]
            made = [(w_new, (i + 1, c, inner(t)), rho[i + 1, c, inner(t)] - alpha * n_vec)]
            if not last:
                made += [(k["z_out"], (i, c, plain(t)), n_vec)]
            return made

        w_now = rho[planes1, col, own_inner]
        m_now = ya[planes1, col, own_inner]
        sweep(ya, rows, z, image, spans[3])
        state, state_out = k["state"], k["state_out"]
        r, u = state[0], state[1]
        p, q, sv = u, m_now, w_now
        if beta is not None:
            p, q, sv = p + beta * state[2], q + beta * state[3], sv + beta * state[4]
            x = state[5] + alpha * p
        else:
            x = alpha * p
        r = r - alpha * sv
        u = u - alpha * q
        w = w_new[planes1, col, own_inner]
        for n, value in enumerate((r, u, p, q, sv, x)):
            state_out[n] = value
        if last:
            state_out[6] = w
        dots = [weighted(r, u, h), weighted(w, u, h), weighted(sv, u, h), weighted(sv, p, h)]

    lane1 = iota((1, LANES), 1)
    line = jnp.zeros((1, LANES), f32)
    for n, value in enumerate(dots):
        line = jnp.where(lane1 == n, value, line)
    out = k["out"]
    if last:
        out[...] = jnp.broadcast_to(line[None], (z.devices, 1, LANES))
        return
    presmooth(w_new, g, k["y2_out"], rows, z)
    restrict_solve(
        w_new, k["y2_out"], g, s, k["hot"], k["inv_t"], k["parts"], k["grouped"], k["msg"], z
    )
    for c in range(z.ngroup):
        out[:, :, c * LANES : (c + 1) * LANES] = jnp.broadcast_to(k["msg"][c][None], (z.devices, 1, LANES))
    lo = z.ngroup * LANES
    out[:, :, lo : lo + LANES] = jnp.broadcast_to(line[None], (z.devices, 1, LANES))


def kernel_last(z, recv, old, state, g, s, x_out, r_out):
    def gather(d, acc):
        return acc + recv[d]

    sums = lax.fori_loop(0, z.devices, gather, jnp.zeros((1, LANES), f32))
    lane1 = iota((1, LANES), 1)
    pick = lambda n: jnp.sum(jnp.where(lane1 == n, sums, 0.0), axis=1, keepdims=True)
    gamma, delta = pick(0), pick(1)
    beta = gamma / old[0:1, 0:1]
    alpha = gamma / (delta + 2.0 * beta * pick(2) + beta * beta * pick(3))
    gx, col = lax.axis_index("gx"), lax.axis_index("col")
    own_rows = slice(HALO, HALO + z.cy)
    for i in range(z.cx):
        gg = g[gx * z.cx + i, col, own_rows]
        ss = s[gx * z.cx + i, col, own_rows]
        p = state[1, i] + beta * state[2, i]
        sv = state[6, i] + beta * state[4, i]
        x_out[i] = (state[5, i] + alpha * p) / ss
        r_out[i] = (state[0, i] - alpha * sv) * (ss / gg)


def call(z, body, outs, scratch, *args, name=None):
    room = 13 * (z.planes + 2) * z.col * z.rows * LANES * 4
    vmem = pl.BlockSpec(memory_space=pltpu.VMEM)
    return pl.pallas_call(
        body,
        out_shape=outs,
        in_specs=[vmem] * len(args),
        out_specs=[vmem] * len(outs),
        scratch_shapes=scratch,
        compiler_params=pltpu.CompilerParams(vmem_limit_bytes=min(room, 60 * 1024 * 1024)),
        name=name,
    )(*args)


def gather_fields(z, fields, inverse):
    cx, n, h = z.cx, 3 * z.cy + 8, 3 * HALO + 8
    shape = lambda *dims: jax.ShapeDtypeStruct(dims, f32)
    names = (fields[3] * z.nblock + fields[4]).astype(f32)
    block = jnp.concatenate(fields[:3] + (jnp.broadcast_to(names, (cx, 8, LANES)),), axis=1)
    edge = shape(cx, h, LANES)
    head, tail, block = call(
        z, functools.partial(kernel_edges, z), [edge, edge, shape(cx, n, LANES)], [], block, name="edges"
    )
    def neighbours():
        above = lax.ppermute(tail, "gy", [(i, i + 1) for i in range(z.gy - 1)])
        return above, lax.ppermute(head, "gy", [(i + 1, i) for i in range(z.gy - 1)])

    flat = lambda value: value.reshape(-1, LANES)

    def turn(value, bit):
        return lax.ppermute(value, "col", [(i, i ^ bit) for i in range(z.col)])

    halo = functools.partial(kernel_halo, z)
    if z.gx == 2:
        swap = lambda value: lax.ppermute(value, "gx", [(0, 1), (1, 0)])
        across, beside = swap(block), turn(block, 2)
        above, below = neighbours()
        above, inverse = lax.optimization_barrier((above, inverse))
        whole = shape(2 * cx * h + cx // 2 * n, LANES)
        to_x, to_y = call(z, halo, [whole, whole], [], above, below, beside, across, name="halo")
        from_x, from_y = swap(to_x), turn(to_y, 2)
        half = cx * h
        corner_low, corner_high = turn(from_x[:half], 2), swap(from_y[half : 2 * half])
        pieces = [flat(block), flat(across), flat(beside), to_x, from_x, from_y, corner_low, corner_high]
        end, cut = 2 * half, cx // 2
        blocks = [(0, 0, 0, 0, cx), (1, 0, 0, cx, cx), (2, 0, 2, 0, cx)]
        blocks += [(5, end, 2, cx, cut), (4, end, 2, cx + cut, cut)]
        halos = [(3, 0, 0, 0, cx), (4, 0, 0, cx, cx), (5, 0, 2, 0, cx)]
        halos += [(6, 0, 2, cx, cut), (7, 0, 2, cx + cut, cut)]
    else:
        above, below = neighbours()
        (edges,) = call(z, halo, [shape(2 * cx * h, LANES)], [], above, below, name="halo")
        pieces = [lax.all_gather(value, "gx", axis=0, tiled=True) for value in (flat(block), edges)]
        pieces += [turn(value, 2) for value in pieces]
        blocks = [(0, 0, 0, 0, z.planes), (2, 0, 2, 0, z.planes)]
        halos = [(1, 0, 0, 0, z.planes), (3, 0, 2, 0, z.planes)]
    count = len(pieces)
    pieces = pieces + [turn(value, 1) for value in pieces]
    mirror = lambda table: table + [(w + count, base, m ^ 1, a, b) for w, base, m, a, b in table]
    return pieces, (mirror(blocks), mirror(halos), 2 * count, z.gx == 2), inverse


def on_device(right_side, diag_shift, stiffness, block_owner, block_group, coarse_inverse):
    cx, cy, depth = right_side.shape
    z = Sizes([lax.axis_size(a) for a in ALL], cx, cy)
    fields = (right_side, diag_shift, stiffness, block_owner, block_group)
    pieces, layout, inv_t = gather_fields(z, fields, jnp.swapaxes(coarse_inverse[0], 1, 2))

    shape = lambda *dims, dtype=f32: jax.ShapeDtypeStruct(dims, dtype)
    field = (z.planes, z.col, z.rows, LANES)
    padded = (z.planes + 2, z.col, z.rows + 2 * PAD, LANES)
    common = [
        pltpu.VMEM((3, z.col, z.cx, z.cy, LANES), f32),
        pltpu.VMEM((z.nblock, LANES), f32),
        pltpu.VMEM((z.ngroup, 1, LANES), f32),
    ]
    g, s, targets, rho, y2, hot, msg = call(
        z,
        functools.partial(kernel_first, z, *layout),
        [
            shape(*field), shape(*field), shape(*field, dtype=jnp.int32), shape(*padded), shape(*padded),
            shape(z.nblock, z.col * LANES, dtype=jnp.bfloat16), shape(z.devices, z.ngroup, LANES),
        ],
        common,
        *pieces, inv_t, name="begin",
    )
    swap = lambda m: lax.all_to_all(m, ALL, split_axis=0, concat_axis=0, tiled=True)
    state = old = z_old = None
    for step in range(ITERS):
        first, last = step == 0, step == ITERS - 1
        recv = swap(msg)
        args = [recv, g, s, targets, rho, y2, hot, inv_t]
        if not first:
            args += [state]
        if step >= 2:
            args += [old, z_old]
        width = (0 if last else z.ngroup * LANES) + LANES
        outs = [shape(7 if last else 6, cx, cy, LANES), shape(z.devices, 1, width)]
        if not last:
            outs += [shape(*padded), shape(*padded)]
        if step >= 1 and not last:
            outs += [shape(*field)]
        if not first:
            outs += [shape(1, LANES)]
        scratch = [pltpu.VMEM((z.devices, z.ngroup, LANES), f32)] + common
        if last:
            scratch += [pltpu.VMEM(padded, f32)] * 2
        result = list(call(z, functools.partial(kernel_next, z, step), outs, scratch, *args, name=f"step{step}"))
        state, msg = result[:2]
        result = result[2:]
        if not last:
            rho, y2 = result[:2]
            result = result[2:]
        if step >= 1 and not last:
            z_old = result.pop(0)
        if not first:
            old = result.pop(0)
        else:
            old = None
    recv = swap(msg)
    x, r = call(
        z,
        functools.partial(kernel_last, z),
        [shape(cx, cy, LANES), shape(cx, cy, LANES)],
        [],
        recv, old, state, g, s, name="end",
    )
    return x, r


def solution(mesh):
    placed = (
        P("gx", "gy", "col"),
        P("gx", "gy", "col"),
        P("gx", "gy", "col"),
        P(("gx", "gy", "col"), None),
        P(("gx", "gy", "col"), None),
        P(("gx", "gy", "col"), None, None, None),
    )
    return jax.shard_map(
        on_device,
        mesh=mesh,
        in_specs=placed,
        out_specs=(P("gx", "gy", "col"), P("gx", "gy", "col")),
        check_vma=False,
    )
```

```python
import functools

import jax
import jax.numpy as jnp
from jax import lax
from jax.experimental import pallas as pl
from jax.experimental.pallas import tpu as pltpu
from jax.sharding import PartitionSpec as P

AGG = 16
ITERS = 4
HALO = 16
LANES = 128
ALL = ("gx", "gy", "col")

w1 = 1.0 / 1.7364
w2 = 1.0 / 0.4636
f32 = jnp.float32


def iota(shape, dim):
    return lax.broadcasted_iota(jnp.int32, shape, dim)


class Sizes:
    def __init__(self, mesh_shape, cx, cy):
        self.gx, self.gy, self.col = mesh_shape
        self.devices = self.gx * self.gy * self.col
        self.cx, self.cy = cx, cy
        self.planes = self.gx * cx
        self.small = self.planes <= 8
        self.rows = cy + 2 * HALO
        self.nblock = cx * cy
        self.ngroup = self.nblock * (LANES // AGG) // LANES


PAD = 8


def plain(t):
    return pl.ds(pl.multiple_of(t * 8, 8), 8)


def inner(t):
    return pl.ds(pl.multiple_of(t * 8 + PAD, 8), 8)


def row_sums(src, i, t, mid, z):
    lane = iota((8, LANES), 1)
    zero = jnp.zeros((8, LANES), f32)
    ahead = [pltpu.roll(x, 1, 1) for x in mid]
    behind = [pltpu.roll(x, LANES - 1, 1) for x in mid]
    out = []
    for c in range(z.col):
        left = jnp.where(lane == 0, ahead[c - 1] if c else zero, ahead[c])
        right = jnp.where(lane == LANES - 1, behind[c + 1] if c + 1 < z.col else zero, behind[c])
        up = src[i, c, pl.ds(t * 8 + PAD - 1, 8)]
        down = src[i, c, pl.ds(t * 8 + PAD + 1, 8)]
        out.append((left + right) + (up + down))
    return out


DELAY = 0


def loop(count, body, unroll):
    if unroll:
        for i in range(count):
            body(i, 0)
    else:
        lax.fori_loop(0, count, body, 0)


class Stores:
    def __init__(self):
        self.waiting = []

    def add(self, *stores):
        self.waiting.append(stores)
        if len(self.waiting) > DELAY:
            self.release()

    def release(self):
        for ref, where, value in self.waiting.pop(0):
            ref[where] = value

    def close(self):
        while self.waiting:
            self.release()


def first_plane(z, span):
    return lax.axis_index("gx") * (z.planes - span) if span else 0


def sweep(src, tiles, z, visit, span=None):
    lo, hi = tiles
    start = first_plane(z, span)
    each = hi - lo if z.small else 1

    def body(turn, carry):
        stores = Stores()
        for part in range(each):
            t = lo + turn * each + part
            load = lambda i: [src[i, c, inner(t)] for c in range(z.col)]
            below, mid = load(start), load(start + 1)
            for k in range(span or z.planes):
                i = start + k
                above = load(i + 2)
                across = row_sums(src, i + 1, t, mid, z)
                made = []
                for c in range(z.col):
                    made += visit(i, t, c, mid[c], across[c] + (below[c] + above[c]))
                stores.add(*made)
                below, mid = mid, above
        stores.close()
        return carry

    lax.fori_loop(0, (hi - lo) // each, body, 0)


def clear_ends(ref, z):
    zero = jnp.zeros(ref.shape[1:], f32)
    ref[0] = zero
    ref[z.planes + 1] = zero


def presmooth(rho, g, out, tiles, z, span=None):
    c0, c1 = w1 * (1.0 - w2) + w2, w1 * w2

    def visit(i, t, c, value, total):
        return [(out, (i + 1, c, inner(t)), c0 * value + (c1 * g[i, c, plain(t)]) * total)]

    sweep(rho, tiles, z, visit, span)


def smooth(src, rho, g, out, w, tiles, z, span=None):
    def visit(i, t, c, value, total):
        moved = rho[i + 1, c, inner(t)] + g[i, c, plain(t)] * total
        return [(out, (i + 1, c, inner(t)), (1.0 - w) * value + w * moved)]

    sweep(src, tiles, z, visit, span)


def restrict_solve(rho, y2, g, s, hot, inv_t, parts, grouped, msg, z):
    first = lax.axis_index("gx") * z.cx
    col = lax.axis_index("col")

    def body(k, carry):
        i = first + k
        stores = Stores()
        for j in range(z.cy // 8):
            t = HALO // 8 + j
            mid = [y2[i + 1, c, inner(t)] for c in range(z.col)]
            across = row_sums(y2, i + 1, t + 0 * k, mid, z)
            made = []
            for c in range(z.col):
                total = across[c] + (y2[i, c, inner(t)] + y2[i + 2, c, inner(t)])
                gg = g[i, c, plain(t)]
                value = (rho[i + 1, c, inner(t)] - mid[c] + gg * total) * (s[i, c, plain(t)] / gg)
                high = value.astype(jnp.bfloat16).astype(f32)
                middle = (value - high).astype(jnp.bfloat16).astype(f32)
                low = value - high - middle
                for n, part in enumerate((high, middle, low)):
                    made += [(parts, (n, c ^ col, k, slice(j * 8, j * 8 + 8)), part)]
            stores.add(*made)
        stores.close()
        return carry

    loop(z.cx, body, z.small)
    total = jnp.zeros((z.nblock, LANES), f32)
    for n in range(3):
        flat = parts[n].reshape(z.col * z.nblock, LANES).astype(jnp.bfloat16)
        total = total + jnp.dot(hot[...], flat, preferred_element_type=f32)
    grouped[...] = total
    per = LANES // AGG
    mask = (iota((per, LANES), 1) // AGG == iota((per, LANES), 0)).astype(f32)

    def solve(c, carry):
        acc = jnp.zeros((per, LANES), f32)
        for half in range(2):
            tile = grouped[pl.ds(c * 16 + half * 8, 8), :]
            for k in range(8):
                value = jnp.broadcast_to(tile[k : k + 1, :], (per, LANES)) * mask
                value = jnp.sum(value, axis=1, keepdims=True)
                acc = acc + value * inv_t[c, (half * 8 + k) * per : (half * 8 + k + 1) * per, :]
        msg[c] = jnp.sum(acc, axis=0, keepdims=True)
        return carry

    loop(z.ngroup, solve, z.small)


def kernel_edges(z, block, head, tail, same):
    h, n = HALO, z.cy
    same[...] = block[...]
    for out, first, extra in ((head, 0, h), (tail, n - h, n - h - 1)):
        for k in range(3):
            out[:, k * h : (k + 1) * h] = block[:, k * n + first : k * n + first + h]
        out[:, 3 * h : 3 * h + 8] = block[:, 3 * n : 3 * n + 8]
        out[:, 3 * h : 3 * h + 1] = block[:, 2 * n + extra : 2 * n + extra + 1]


def kernel_halo(z, above, below, *refs):
    m = above.shape[1]
    outs = refs[len(refs) // 2 :] if len(refs) > 1 else refs
    blocks = refs[: len(refs) // 2] if len(refs) > 1 else ()
    for out in outs:
        for i in range(z.cx):
            out[2 * m * i : 2 * m * i + m] = above[i]
            out[2 * m * i + m : 2 * m * (i + 1)] = below[i]
    for out, block, first in zip(outs, blocks, (z.cx // 2, 0)):
        base, n = 2 * m * z.cx, block.shape[1]
        for k in range(z.cx // 2):
            out[base + k * n : base + (k + 1) * n] = block[first + k]


def kernel_first(z, blocks, halos, count, rotated, *refs):
    pieces = refs[:count]
    refs = refs[count:]
    inv_t, g, s, targets, rho, y2, hot, out = refs[:8]
    parts, grouped, msg = refs[8:]
    wide = y2
    gx, col = lax.axis_index("gx"), lax.axis_index("col")
    clear_ends(rho, z)
    clear_ends(y2, z)
    r = z.rows
    tiles = (0, r // 8)

    n, h = z.cy, HALO
    group = iota((z.nblock, LANES), 0).astype(f32) + (col * z.nblock).astype(f32)

    def place(p):
        if not rotated:
            return p
        i = p + gx * z.cx
        return jnp.where(i >= z.planes, i - z.planes, i)

    def spread(names, i, c, p, first, rows, at):
        shape = (rows, LANES)
        wanted = iota(shape, 1) == iota(shape, 0) + ((p % z.cx) * n + first)
        value = jnp.sum(jnp.where(wanted, jnp.broadcast_to(names, shape), 0.0), axis=1, keepdims=True)
        targets[i, c, at : at + rows] = jnp.broadcast_to(value, shape).astype(jnp.int32)

    for which, base, m, start, planes in blocks:

        def each(q, carry, piece=pieces[which], base=base, m=m, start=start):
            p = q + start
            i, c, row = place(p), col ^ m, base + q * (3 * n + 8)
            rho[i + 1, c, PAD + h : PAD + h + n] = piece[pl.ds(row, n)]
            g[i, c, h : h + n] = piece[pl.ds(row + n, n)]
            wide[i + 1, c, PAD + h : PAD + h + n] = piece[pl.ds(row + 2 * n, n)]
            spread(piece[pl.ds(row + 3 * n, 1)], i, c, p, 0, n, h)
            return carry

        loop(planes, each, z.small)
        if start == 0:
            shift = 0 if rotated else gx * (z.cx * (3 * n + 8))
            names = jnp.broadcast_to(pieces[which][pl.ds(base + shift + 3 * n, 1)], (z.nblock, LANES))
            hot[:, m * LANES : (m + 1) * LANES] = (names == group).astype(jnp.bfloat16)

    for which, base, m, start, planes in halos:

        def each(q, carry, piece=pieces[which], base=base, m=m, start=start):
            p = q + start
            i, c, row = place(p), col ^ m, base + q * (6 * h + 16)
            for top, first, edge, turn in ((row, 0, PAD - 1, n - h), (row + 3 * h + 8, h + n, PAD + r, 0)):
                rho[i + 1, c, PAD + first : PAD + first + h] = piece[pl.ds(top, h)]
                g[i, c, first : first + h] = piece[pl.ds(top + h, h)]
                wide[i + 1, c, PAD + first : PAD + first + h] = piece[pl.ds(top + 2 * h, h)]
                wide[i + 1, c, edge : edge + 1] = piece[pl.ds(top + 3 * h, 1)]
                spread(piece[pl.ds(top + 3 * h + 1, 1)], i, c, p, turn, h, first)
            return carry

        loop(planes, each, z.small)

    def coefficients(i, t, c, x, total):
        diagonal = g[i, c, plain(t)] + x * total
        inside = diagonal > 0.0
        scale = jnp.where(inside, x / jnp.where(inside, diagonal, 1.0), 0.0)
        return [
            (s, (i, c, plain(t)), x),
            (g, (i, c, plain(t)), x * scale),
            (rho, (i + 1, c, inner(t)), rho[i + 1, c, inner(t)] * scale),
        ]

    sweep(wide, tiles, z, coefficients)
    presmooth(rho, g, y2, tiles, z)
    restrict_solve(rho, y2, g, s, hot, inv_t, parts, grouped, msg, z)
    for c in range(z.ngroup):
        out[:, c : c + 1, :] = jnp.broadcast_to(msg[c][None], (z.devices, 1, LANES))


def prolong(recv, table, y2, s, targets, out, tiles, z, packed, span=None):
    n = z.ngroup
    if packed:

        def unpack(d, carry):
            for c in range(n):
                table[d, c : c + 1, :] = recv[d, :, c * LANES : (c + 1) * LANES]
            return carry

        loop(z.devices, unpack, z.small)
    else:
        table = recv
    gy = lax.axis_index("gy")
    aggregate = iota((8, LANES), 1) // AGG

    tiles = tuple(range(tiles[0], tiles[1]))

    start = first_plane(z, span)

    def body(k, carry):
        i = start + k
        gx = i // z.cx
        stores = Stores()
        for tile in tiles:
            side = -1 if tile * 8 < HALO else (1 if tile * 8 >= HALO + z.cy else 0)
            layer = jnp.clip(gy + side, 0, z.gy - 1)
            base = (gx * z.gy + layer) * z.col
            tables = [table[base + o] for o in range(z.col)]
            made = []
            for c in range(z.col):
                t = targets[i, c, plain(tile)]
                line = t >> 4
                owner, block = line >> 3, line & 7
                picked = jnp.take_along_axis(tables[0], block, axis=0, mode="promise_in_bounds")
                for o in range(1, z.col):
                    other = jnp.take_along_axis(tables[o], block, axis=0, mode="promise_in_bounds")
                    picked = jnp.where(owner == o, other, picked)
                lane = (t & 15) * 8 + aggregate
                picked = jnp.take_along_axis(picked, lane, axis=1, mode="promise_in_bounds")
                value = y2[i + 1, c, inner(tile)] + s[i, c, plain(tile)] * picked
                made += [(out, (i + 1, c, inner(tile)), value)]
            stores.add(*made)
        stores.close()
        return carry

    loop(span or z.planes, body, z.small)


def weighted(a, b, h):
    return jnp.sum(jnp.sum(a * b * h, axis=(0, 1), keepdims=True)[0], axis=1, keepdims=True)


def kernel_next(z, step, *refs):
    first, last = step == 0, step == ITERS - 1
    names = ["recv", "g", "s", "targets", "rho", "y2", "hot", "inv_t"]
    if not first:
        names += ["state"]
    if step >= 2:
        names += ["old", "z_old"]
    outs = ["state_out", "out"]
    if not last:
        outs += ["w_out", "y2_out"]
    if step >= 1 and not last:
        outs += ["z_out"]
    if not first:
        outs += ["old_out"]
    scratch = ["table", "parts", "grouped", "msg"] + (["y2_out", "w_out"] if last else [])
    k = dict(zip(names + outs + scratch, refs))
    g, s, rho = k["g"], k["s"], k["rho"]
    ya, yb, table = k["y2_out"], k["w_out"], k["table"]
    clear_ends(ya, z)
    clear_ends(yb, z)
    trim = 1 if step >= 1 else 0
    rows = (trim, z.rows // 8 - trim)
    early = (0, z.rows // 8) if step <= 1 else rows
    spans = [None] * 4
    if last:
        rows = (HALO // 8, (HALO + z.cy) // 8)
        if z.gx == 2 and z.cx > 3:
            spans = [z.cx + n for n in (3, 2, 1, 0)]
    prolong(k["recv"], table, k["y2"], s, k["targets"], ya, early, z, not first, spans[0])
    smooth(ya, rho, g, yb, w2, early, z, spans[1])
    smooth(yb, rho, g, ya, w1, early, z, spans[2])

    gx, col = lax.axis_index("gx"), lax.axis_index("col")
    own_rows = slice(HALO, HALO + z.cy)
    own_inner = slice(HALO + PAD, HALO + PAD + z.cy)
    planes = pl.ds(gx * z.cx, z.cx)
    planes1 = pl.ds(gx * z.cx + 1, z.cx)
    h = 1.0 / g[planes, col, own_rows]
    w_new = yb
    if first:

        def image(i, t, c, value, total):
            return [(w_new, (i + 1, c, inner(t)), value - g[i, c, plain(t)] * total)]

        sweep(ya, rows, z, image)
        r, u, w = (ref[planes1, col, own_inner] for ref in (rho, ya, w_new))
        k["state_out"][0] = r
        k["state_out"][1] = u
        dots = [weighted(r, u, h), weighted(w, u, h)]
    else:
        sums = jnp.zeros((1, LANES), f32)
        lo = z.ngroup * LANES

        def gather(d, acc):
            return acc + k["recv"][d, :, lo : lo + LANES]

        sums = lax.fori_loop(0, z.devices, gather, sums)
        lane1 = iota((1, LANES), 1)
        pick = lambda n: jnp.sum(jnp.where(lane1 == n, sums, 0.0), axis=1, keepdims=True)
        gamma, delta = pick(0), pick(1)
        k["old_out"][...] = jnp.broadcast_to(gamma, (1, LANES))
        if step == 1:
            beta = None
            alpha = gamma / delta
        else:
            beta = gamma / k["old"][0:1, 0:1]
            alpha = gamma / (delta + 2.0 * beta * pick(2) + beta * beta * pick(3))

        def image(i, t, c, value, total):
            n_vec = value - g[i, c, plain(t)] * total
            if beta is not None:
                n_vec = n_vec + beta * k["z_old"][i, c, plain(t)]
            made = [(w_new, (i + 1, c, inner(t)), rho[i + 1, c, inner(t)] - alpha * n_vec)]
            if not last:
                made += [(k["z_out"], (i, c, plain(t)), n_vec)]
            return made

        w_now = rho[planes1, col, own_inner]
        m_now = ya[planes1, col, own_inner]
        sweep(ya, rows, z, image, spans[3])
        state, state_out = k["state"], k["state_out"]
        r, u = state[0], state[1]
        p, q, sv = u, m_now, w_now
        if beta is not None:
            p, q, sv = p + beta * state[2], q + beta * state[3], sv + beta * state[4]
            x = state[5] + alpha * p
        else:
            x = alpha * p
        r = r - alpha * sv
        u = u - alpha * q
        w = w_new[planes1, col, own_inner]
        for n, value in enumerate((r, u, p, q, sv, x)):
            state_out[n] = value
        if last:
            state_out[6] = w
        dots = [weighted(r, u, h), weighted(w, u, h), weighted(sv, u, h), weighted(sv, p, h)]

    lane1 = iota((1, LANES), 1)
    line = jnp.zeros((1, LANES), f32)
    for n, value in enumerate(dots):
        line = jnp.where(lane1 == n, value, line)
    out = k["out"]
    if last:
        out[...] = jnp.broadcast_to(line[None], (z.devices, 1, LANES))
        return
    ends = step == ITERS - 2 and z.gx == 2 and z.cx > 3
    presmooth(w_new, g, k["y2_out"], rows, z, z.cx + 3 if ends else None)
    restrict_solve(
        w_new, k["y2_out"], g, s, k["hot"], k["inv_t"], k["parts"], k["grouped"], k["msg"], z
    )
    for c in range(z.ngroup):
        out[:, :, c * LANES : (c + 1) * LANES] = jnp.broadcast_to(k["msg"][c][None], (z.devices, 1, LANES))
    lo = z.ngroup * LANES
    out[:, :, lo : lo + LANES] = jnp.broadcast_to(line[None], (z.devices, 1, LANES))


def kernel_last(z, recv, old, state, g, s, x_out, r_out):
    def gather(d, acc):
        return acc + recv[d]

    sums = lax.fori_loop(0, z.devices, gather, jnp.zeros((1, LANES), f32))
    lane1 = iota((1, LANES), 1)
    pick = lambda n: jnp.sum(jnp.where(lane1 == n, sums, 0.0), axis=1, keepdims=True)
    gamma, delta = pick(0), pick(1)
    beta = gamma / old[0:1, 0:1]
    alpha = gamma / (delta + 2.0 * beta * pick(2) + beta * beta * pick(3))
    gx, col = lax.axis_index("gx"), lax.axis_index("col")
    own_rows = slice(HALO, HALO + z.cy)
    for i in range(z.cx):
        gg = g[gx * z.cx + i, col, own_rows]
        ss = s[gx * z.cx + i, col, own_rows]
        p = state[1, i] + beta * state[2, i]
        sv = state[6, i] + beta * state[4, i]
        x_out[i] = (state[5, i] + alpha * p) / ss
        r_out[i] = (state[0, i] - alpha * sv) * (ss / gg)


def call(z, body, outs, scratch, *args, name=None):
    room = 13 * (z.planes + 2) * z.col * z.rows * LANES * 4
    vmem = pl.BlockSpec(memory_space=pltpu.VMEM)
    return pl.pallas_call(
        body,
        out_shape=outs,
        in_specs=[vmem] * len(args),
        out_specs=[vmem] * len(outs),
        scratch_shapes=scratch,
        compiler_params=pltpu.CompilerParams(vmem_limit_bytes=min(room, 60 * 1024 * 1024)),
        name=name,
    )(*args)


def gather_fields(z, fields, inverse):
    cx, n, h = z.cx, 3 * z.cy + 8, 3 * HALO + 8
    shape = lambda *dims: jax.ShapeDtypeStruct(dims, f32)
    names = (fields[3] * z.nblock + fields[4]).astype(f32)
    block = jnp.concatenate(fields[:3] + (jnp.broadcast_to(names, (cx, 8, LANES)),), axis=1)
    edge = shape(cx, h, LANES)
    head, tail, block = call(
        z, functools.partial(kernel_edges, z), [edge, edge, shape(cx, n, LANES)], [], block, name="edges"
    )
    def neighbours():
        above = lax.ppermute(tail, "gy", [(i, i + 1) for i in range(z.gy - 1)])
        return above, lax.ppermute(head, "gy", [(i + 1, i) for i in range(z.gy - 1)])

    flat = lambda value: value.reshape(-1, LANES)

    def turn(value, bit):
        return lax.ppermute(value, "col", [(i, i ^ bit) for i in range(z.col)])

    halo = functools.partial(kernel_halo, z)
    if z.gx == 2:
        swap = lambda value: lax.ppermute(value, "gx", [(0, 1), (1, 0)])
        across, beside = swap(block), turn(block, 2)
        above, below = neighbours()
        above, inverse = lax.optimization_barrier((above, inverse))
        whole = shape(2 * cx * h + cx // 2 * n, LANES)
        to_x, to_y = call(z, halo, [whole, whole], [], above, below, beside, across, name="halo")
        from_x, from_y = swap(to_x), turn(to_y, 2)
        half = cx * h
        corner_low, corner_high = turn(from_x[:half], 2), swap(from_y[half : 2 * half])
        pieces = [flat(block), flat(across), flat(beside), to_x, from_x, from_y, corner_low, corner_high]
        end, cut = 2 * half, cx // 2
        blocks = [(0, 0, 0, 0, cx), (1, 0, 0, cx, cx), (2, 0, 2, 0, cx)]
        blocks += [(5, end, 2, cx, cut), (4, end, 2, cx + cut, cut)]
        halos = [(3, 0, 0, 0, cx), (4, 0, 0, cx, cx), (5, 0, 2, 0, cx)]
        halos += [(6, 0, 2, cx, cut), (7, 0, 2, cx + cut, cut)]
    else:
        above, below = neighbours()
        (edges,) = call(z, halo, [shape(2 * cx * h, LANES)], [], above, below, name="halo")
        pieces = [lax.all_gather(value, "gx", axis=0, tiled=True) for value in (flat(block), edges)]
        pieces += [turn(value, 2) for value in pieces]
        blocks = [(0, 0, 0, 0, z.planes), (2, 0, 2, 0, z.planes)]
        halos = [(1, 0, 0, 0, z.planes), (3, 0, 2, 0, z.planes)]
    count = len(pieces)
    pieces = pieces + [turn(value, 1) for value in pieces]
    mirror = lambda table: table + [(w + count, base, m ^ 1, a, b) for w, base, m, a, b in table]
    return pieces, (mirror(blocks), mirror(halos), 2 * count, z.gx == 2), inverse


def on_device(right_side, diag_shift, stiffness, block_owner, block_group, coarse_inverse):
    cx, cy, depth = right_side.shape
    z = Sizes([lax.axis_size(a) for a in ALL], cx, cy)
    fields = (right_side, diag_shift, stiffness, block_owner, block_group)
    pieces, layout, inv_t = gather_fields(z, fields, jnp.swapaxes(coarse_inverse[0], 1, 2))

    shape = lambda *dims, dtype=f32: jax.ShapeDtypeStruct(dims, dtype)
    field = (z.planes, z.col, z.rows, LANES)
    padded = (z.planes + 2, z.col, z.rows + 2 * PAD, LANES)
    common = [
        pltpu.VMEM((3, z.col, z.cx, z.cy, LANES), f32),
        pltpu.VMEM((z.nblock, LANES), f32),
        pltpu.VMEM((z.ngroup, 1, LANES), f32),
    ]
    g, s, targets, rho, y2, hot, msg = call(
        z,
        functools.partial(kernel_first, z, *layout),
        [
            shape(*field), shape(*field), shape(*field, dtype=jnp.int32), shape(*padded), shape(*padded),
            shape(z.nblock, z.col * LANES, dtype=jnp.bfloat16), shape(z.devices, z.ngroup, LANES),
        ],
        common,
        *pieces, inv_t, name="begin",
    )
    swap = lambda m: lax.all_to_all(m, ALL, split_axis=0, concat_axis=0, tiled=True)
    state = old = z_old = None
    for step in range(ITERS):
        first, last = step == 0, step == ITERS - 1
        recv = swap(msg)
        args = [recv, g, s, targets, rho, y2, hot, inv_t]
        if not first:
            args += [state]
        if step >= 2:
            args += [old, z_old]
        width = (0 if last else z.ngroup * LANES) + LANES
        outs = [shape(7 if last else 6, cx, cy, LANES), shape(z.devices, 1, width)]
        if not last:
            outs += [shape(*padded), shape(*padded)]
        if step >= 1 and not last:
            outs += [shape(*field)]
        if not first:
            outs += [shape(1, LANES)]
        scratch = [pltpu.VMEM((z.devices, z.ngroup, LANES), f32)] + common
        if last:
            scratch += [pltpu.VMEM(padded, f32)] * 2
        result = list(call(z, functools.partial(kernel_next, z, step), outs, scratch, *args, name=f"step{step}"))
        state, msg = result[:2]
        result = result[2:]
        if not last:
            rho, y2 = result[:2]
            result = result[2:]
        if step >= 1 and not last:
            z_old = result.pop(0)
        if not first:
            old = result.pop(0)
        else:
            old = None
    recv = swap(msg)
    x, r = call(
        z,
        functools.partial(kernel_last, z),
        [shape(cx, cy, LANES), shape(cx, cy, LANES)],
        [],
        recv, old, state, g, s, name="end",
    )
    return x, r


def solution(mesh):
    placed = (
        P("gx", "gy", "col"),
        P("gx", "gy", "col"),
        P("gx", "gy", "col"),
        P(("gx", "gy", "col"), None),
        P(("gx", "gy", "col"), None),
        P(("gx", "gy", "col"), None, None, None),
    )
    return jax.shard_map(
        on_device,
        mesh=mesh,
        in_specs=placed,
        out_specs=(P("gx", "gy", "col"), P("gx", "gy", "col")),
        check_vma=False,
    )
```
